32 devices in a mesh: groups: 2 (over y), blk: 16 (over z, x, core).
Axes of the slice: x: 2, y: 2, z: 4, core: 2. Of those that a mesh axis runs over, the one named last changes fastest.
Arguments:
- ensemble: bfloat16 [256, 131072], P(None, ('groups', 'blk')), parts along dimension 1, may hold values from -6 to 6
- predicted: bfloat16 [256, 4096], P(None, ('groups', 'blk')), parts along dimension 1, may hold values from -6 to 6
- targets: bfloat16 [256, 4096], P(None, ('groups', 'blk')), parts along dimension 1, may hold values from -9 to 9
- datum_noise_variance: float32 [4096], P(('groups', 'blk')), parts along dimension 0, may hold values from 0.16 to 2, as said below
- block_ids: int32 [32], P('groups'), parts along dimension 0, may hold values from 0 to 15, each once
- pair_blocks: int32 [512, 16], P(('groups', 'blk')), parts along dimension 0, may hold values from 0 to 15
- taper: float32 [512, 16], P(('groups', 'blk')), parts along dimension 0, may hold values from 0.2 to 1
Outputs:
- ensemble_step: float32 [256, 131072], P(None, ('groups', 'blk')), parts along dimension 1
The draws below stay inside these ranges and needn't reach their ends.
There are 2 independent parts, one for each index of `groups`. The reference program is written for one: setup_inputs(seed, part) draws one part's arguments, and reference() takes and returns one part's arrays. A program takes and returns all parts, laid end to end along the dimension named above; each array names one. Nothing has to cross between parts.
Inputs may be any that keep to these rules, and one draw needn't show every extreme that they name: `datum_noise_variance`: a variance that falls threefold from the first datum to the last, times an independent factor between 0.5 and 2, clipped to the range. `block_ids`: each data block is held in exactly one slot.
All inputs are finite; a program needn't handle non-finite values.
Results may differ from the reference program's by a relative error of at most 0.033.
Values may be sent and summed in bfloat16 or wider, within the bound.
A program may use at most 128 MiB of HBM per device.

```python
import math
import jax
import jax.numpy as jnp
from jax import lax

BLOCK = 256
DATA_PER_BLOCK = 128
MEM = 256
PAIRS = 16
BLOCK_COUNT = 16
NC = 256
CELLS = 65536
DATA = 2048


def shared_patterns(key):
    factor_count = 32
    pattern_key = jax.random.fold_in(key, 7331)
    base_key = jax.random.fold_in(key, 7919)
    weight_key = jax.random.fold_in(key, 8623)
    patterns = jax.random.normal(pattern_key, (factor_count, DATA), jnp.float32)
    base_field = 0.6 * jax.random.normal(base_key, (DATA,), jnp.float32)
    truth_weights = jax.random.normal(weight_key, (factor_count,), jnp.float32)
    strengths = 0.6 * jnp.exp(-math.log(100.0) * jnp.arange(factor_count, dtype=jnp.float32) / (factor_count - 1.0))
    return (patterns, base_field, truth_weights, strengths)


def draw_predicted(key, part):
    patterns, base_field, truth_weights, strengths = shared_patterns(key)
    factor_count = patterns.shape[0]
    member_key = jax.random.fold_in(key, 4409)
    noise_key = jax.random.fold_in(key, 5113)
    member_factors = jax.random.normal(member_key, (MEM, factor_count), jnp.float32)
    noise_values = jax.random.normal(noise_key, (MEM, DATA), jnp.float32)
    field = base_field[None, :] + 0.2 * noise_values
    for factor_index in range(factor_count):
        column = member_factors[:, factor_index:factor_index + 1] * strengths[factor_index]
        field = field + column * patterns[factor_index][None, :]
    return jnp.clip(field, -6.0, 6.0).astype(jnp.bfloat16)


def draw_targets(key, part):
    patterns, base_field, truth_weights, strengths = shared_patterns(key)
    factor_count = patterns.shape[0]
    perturb_key = jax.random.fold_in(key, 6271)
    perturbation = jax.random.normal(perturb_key, (MEM, DATA), jnp.float32)
    observed = base_field
    for factor_index in range(factor_count):
        observed = observed + truth_weights[factor_index] * strengths[factor_index] * patterns[factor_index]
    field = observed[None, :] + 0.7 * perturbation
    return jnp.clip(field, -9.0, 9.0).astype(jnp.bfloat16)


def draw_datum_noise_variance(key, part):
    position = jnp.arange(DATA, dtype=jnp.float32) / DATA
    ramp = jnp.exp(-jnp.log(3.0) * position)
    factor = jnp.exp(jax.random.uniform(key, (DATA,), jnp.float32, jnp.log(0.5), jnp.log(2.0)))
    return jnp.clip(ramp * factor, 0.16, 2.0).astype(jnp.float32)


def place_ends(array, rng, low, largest):
    longest = array.shape.index(max(array.shape))
    spots = []
    for shift in (0, 1):
        where = [jax.random.randint(jax.random.fold_in(rng, axis), (), 0, length) for axis, length in enumerate(array.shape)]
        where[longest] = (where[longest] + shift) % array.shape[longest]
        spots.append(tuple(where))
    return array.at[spots[0]].set(low).at[spots[1]].set(largest)


def steps_of(key, dims, cuts, low, largest):
    def one(axis_at, parts):
        steps = jax.random.uniform(jax.random.fold_in(jax.random.fold_in(key, 6), axis_at), (parts,), jnp.float32, low / len(cuts), largest / len(cuts))
        return jnp.repeat(jnp.exp(steps), dims[axis_at] // parts).reshape((-1,) + (1,) * (len(dims) - axis_at - 1))

    level = one(*cuts[0])
    for cut in cuts[1:]:
        level = level * one(*cut)
    return level


def gaussian(rng, dims, width, limit, pieces=(), held_as=jnp.bfloat16):
    level = steps_of(rng, dims, pieces, -0.22, 0.18) if pieces else 1.0
    entries = jax.random.normal(rng, dims, jnp.float32) * width * level
    return jnp.minimum(jnp.maximum(entries, -limit), limit).astype(held_as)


def setup_inputs(seed: int = 0, part: int = 0) -> dict:
    keys = jax.random.split(jax.random.key(seed), 8)
    own_keys = jax.random.split(jax.random.fold_in(keys[7], part), 8)
    ensemble = gaussian(own_keys[0], (MEM, CELLS), 1.0, 6.0, ((1, 16),))
    predicted = draw_predicted(jax.random.fold_in(jax.random.fold_in(keys[7], part), 71), part)
    targets = draw_targets(jax.random.fold_in(jax.random.fold_in(keys[7], part), 71), part)
    datum_noise_variance = draw_datum_noise_variance(jax.random.fold_in(jax.random.fold_in(keys[7], part), 71), part)
    block_ids = jax.random.permutation(own_keys[4], BLOCK_COUNT).astype(jnp.int32)
    pair_blocks = place_ends(jax.random.randint(own_keys[5], (NC, PAIRS), 0, BLOCK_COUNT), jax.random.fold_in(own_keys[5], 1), 0, BLOCK_COUNT - 1).astype(jnp.int32)
    taper = jnp.clip(0.2 + 0.8 * jax.random.uniform(own_keys[6], (NC, PAIRS), jnp.float32) ** steps_of(own_keys[6], (NC, PAIRS), ((0, 16),), -0.2, 0.2), 0.2, 1.0)
    return {"ensemble": ensemble, "predicted": predicted, "targets": targets, "datum_noise_variance": datum_noise_variance, "block_ids": block_ids, "pair_blocks": pair_blocks, "taper": taper}


def chol_solve(zmat, rhs):
    factor = jnp.linalg.cholesky(zmat)
    lower_part = lax.linalg.triangular_solve(factor, rhs, left_side=True, lower=True)
    return lax.linalg.triangular_solve(factor, lower_part, left_side=True, lower=True, transpose_a=True)

def reference(ensemble, predicted, targets, datum_noise_variance, block_ids, pair_blocks, taper):
    single_float = jnp.float32
    ensemble_members = ensemble.shape[0]
    uanom = (ensemble.astype(single_float) - jnp.mean(ensemble.astype(single_float), axis=0)).astype(jnp.bfloat16)
    data_deviation = (predicted.astype(single_float) - jnp.mean(predicted.astype(single_float), axis=0)).astype(jnp.bfloat16)
    resid_full = targets.astype(single_float) - predicted.astype(single_float)
    residual_misfit = resid_full.astype(jnp.bfloat16)
    scaled = (data_deviation.astype(single_float) / datum_noise_variance).astype(jnp.bfloat16)
    gram = jnp.dot(scaled, data_deviation.T, preferred_element_type=single_float)
    cross = jnp.dot(scaled, residual_misfit.T, preferred_element_type=single_float)
    zmat = gram + (ensemble_members - 1.0) * jnp.eye(ensemble_members, dtype=single_float)
    xmat = chol_solve(zmat, cross)
    update_term = jnp.dot(xmat.T, data_deviation.astype(single_float), precision=lax.Precision.HIGHEST)
    solved_matrix = ((residual_misfit.astype(single_float) - update_term) / datum_noise_variance).astype(jnp.bfloat16)
    dblocks = data_deviation.astype(single_float).reshape(ensemble_members, BLOCK_COUNT, DATA_PER_BLOCK)
    solved_blocks = solved_matrix.astype(single_float).reshape(ensemble_members, BLOCK_COUNT, DATA_PER_BLOCK)
    gains = (jnp.einsum('ikd,jkd->kij', dblocks, solved_blocks) / (ensemble_members - 1.0)).astype(jnp.bfloat16)
    flat_gains = gains.astype(single_float).reshape(BLOCK_COUNT, ensemble_members * ensemble_members)
    match = (pair_blocks[:, :, None] == block_ids[None, None, :]).astype(single_float)
    weight = jnp.sum(taper[:, :, None] * match, axis=1)
    ublocks = jnp.transpose(uanom.reshape(ensemble_members, NC, BLOCK), (1, 0, 2))

    def one_block(item):
        wrow, ublock = item
        gsum = jnp.dot(wrow, flat_gains, precision=lax.Precision.HIGHEST)
        gsum = gsum.reshape(ensemble_members, ensemble_members).astype(jnp.bfloat16)
        return jnp.dot(gsum.T, ublock, preferred_element_type=single_float)
    result = lax.map(one_block, (weight, ublocks))
    return jnp.transpose(result, (1, 0, 2)).reshape(ensemble_members, NC * BLOCK)
```

```python
import functools

import jax
import jax.numpy as jnp
from jax import lax
from jax.experimental import pallas as pl
from jax.experimental.pallas import tpu as pltpu
from jax.sharding import PartitionSpec as P

MESH = pl.DeviceIdType.MESH
F32 = jnp.float32
BF16 = jnp.bfloat16
NT = (((1,), (1,)), ((), ()))
TILE = 128
STRIP = 16
ROWS = 16


def chip_grid(n):
    chips = n // 2
    nx = max(f for f in range(1, chips + 1) if chips % f == 0 and f * f * f <= chips)
    return chips // nx, nx


def gather_kernel(
    nz, nx, pred, targ, var, dev, res, var_row, gram, cross,
    buf, vbuf, local_sem, send_sem, vsend_sem, recv_sem, vrecv_sem,
):
    width = buf.shape[-1]
    me = lax.axis_index("blk")
    core = me % 2
    x = (me // 2) % nx
    z = me // (2 * nx)
    exists = (z < nz - 1, z > 0, x < nx - 1, x > 0, core >= 0)
    target = (me + 2 * nx, me - 2 * nx, me + 2, me - 2, me + 1 - 2 * core)

    local = (
        pltpu.make_async_copy(pred, buf.at[me, 0], local_sem.at[0]),
        pltpu.make_async_copy(targ, buf.at[me, 1], local_sem.at[1]),
        pltpu.make_async_copy(var, vbuf.at[me], local_sem.at[2]),
    )
    for copy in local:
        copy.start()
    barrier = pltpu.get_barrier_semaphore()
    for d in range(5):
        @pl.when(exists[d])
        def _(d=d):
            pl.semaphore_signal(barrier, inc=1, device_id={"blk": target[d]}, device_id_type=MESH)
    pl.semaphore_wait(barrier, sum(e.astype(jnp.int32) for e in exists))
    gram[...] = jnp.zeros_like(gram)
    cross[...] = jnp.zeros_like(cross)
    for copy in local:
        copy.wait()

    def copies(o, d, h):
        made = [
            pltpu.make_async_remote_copy(
                src_ref=buf.at[o, h], dst_ref=buf.at[o, h], send_sem=send_sem.at[d, h, o],
                recv_sem=recv_sem.at[h, o], device_id={"blk": target[d]}, device_id_type=MESH,
            )
        ]
        if h == 0:
            made.append(
                pltpu.make_async_remote_copy(
                    src_ref=vbuf.at[o], dst_ref=vbuf.at[o], send_sem=vsend_sem.at[d, o],
                    recv_sem=vrecv_sem.at[o], device_id={"blk": target[d]}, device_id_type=MESH,
                )
            )
        return made

    def send(cond, o, d, h):
        @pl.when(cond)
        def _():
            for copy in copies(o, d, h):
                copy.start()

    def arrive(o, h):
        for copy in copies(o, 4, h):
            copy.wait_recv()

    def compute(o):
        p = buf[o, 0].astype(F32)
        t = buf[o, 1].astype(F32)
        v = vbuf[o]
        dd = p - jnp.mean(p, axis=0, keepdims=True)
        db = dd.astype(BF16)
        rb = (t - p).astype(BF16)
        sb = (db.astype(F32) / v).astype(BF16)
        cols = pl.ds(pl.multiple_of(o * width, width), width)
        dev[:, cols] = db
        res[:, cols] = rb
        var_row[:, cols] = v
        gram[...] += lax.dot_general(sb, db, NT, preferred_element_type=F32)
        cross[...] += lax.dot_general(sb, rb, NT, preferred_element_type=F32)

    def lagged(t, lag):
        d = t // 2 - lag
        s = 1 - 2 * (t % 2)
        zo = z - s * d
        valid = (d >= 0) & (zo >= 0) & (zo < nz) & ((d > 0) | (s == 1))
        return d, s, zo, valid

    def step(t, carry):
        d, s, zo, valid = lagged(t, 0)

        @pl.when(valid)
        def _():
            o = (zo * nx + x) * 2 + core

            for h in range(2):
                @pl.when(d > 0)
                def _(h=h):
                    arrive(o, h)
                send(((d == 0) | (s == 1)) & exists[0], o, 0, h)
                send(((d == 0) | (s == -1)) & exists[1], o, 1, h)
                send(exists[2], o, 2, h)
                send(exists[3], o, 3, h)
                send(exists[4], o, 4, h)

        _, _, zx, valid_x = lagged(t, 1)

        @pl.when(valid_x)
        def _():
            def over_x(xo, carry):
                @pl.when(xo != x)
                def _():
                    o = (zx * nx + xo) * 2 + core
                    for h in range(2):
                        arrive(o, h)
                        send((xo < x) & exists[2], o, 2, h)
                        send((xo > x) & exists[3], o, 3, h)
                        send(exists[4], o, 4, h)
                return carry
            lax.fori_loop(0, nx, over_x, 0)

        @pl.when(valid)
        def _():
            compute((zo * nx + x) * 2 + core)

        @pl.when(valid_x)
        def _():
            def over_x(xo, carry):
                @pl.when(xo != x)
                def _():
                    compute((zx * nx + xo) * 2 + core)
                return carry
            lax.fori_loop(0, nx, over_x, 0)

        _, _, zp, valid_p = lagged(t, 2)

        @pl.when(valid_p)
        def _():
            def over_x(xo, carry):
                o = (zp * nx + xo) * 2 + 1 - core
                arrive(o, 0)
                arrive(o, 1)
                compute(o)
                return carry
            lax.fori_loop(0, nx, over_x, 0)
        return carry

    lax.fori_loop(0, 2 * (nz + 2), step, 0)

    def drain(k, carry):
        zo = k // nx
        xo = k % nx
        o = k * 2 + core
        sent = (
            (xo == x) & (zo <= z) & exists[0],
            (xo == x) & (zo >= z) & exists[1],
            (xo <= x) & exists[2],
            (xo >= x) & exists[3],
            exists[4],
        )
        for d in range(5):
            @pl.when(sent[d])
            def _(d=d):
                for copy in copies(o, d, 0) + copies(o, d, 1):
                    copy.wait_send()
        return carry

    lax.fori_loop(0, nz * nx, drain, 0)


def gather(n, pred, targ, var):
    nz, nx = chip_grid(n)
    members, width = pred.shape
    hbm = pl.BlockSpec(memory_space=pl.ANY)
    vmem = pl.BlockSpec(memory_space=pltpu.VMEM)
    sem = pltpu.SemaphoreType.DMA
    return pl.pallas_call(
        functools.partial(gather_kernel, nz, nx),
        out_shape=(
            jax.ShapeDtypeStruct((members, n * width), BF16),
            jax.ShapeDtypeStruct((members, n * width), BF16),
            jax.ShapeDtypeStruct((1, n * width), F32),
            jax.ShapeDtypeStruct((members, members), F32),
            jax.ShapeDtypeStruct((members, members), F32),
        ),
        in_specs=[hbm, hbm, hbm],
        out_specs=(vmem,) * 5,
        scratch_shapes=[
            pltpu.VMEM((n, 2, members, width), BF16),
            pltpu.VMEM((n, 1, width), F32),
            sem((3,)), sem((5, 2, n)), sem((5, n)), sem((2, n)), sem((n,)),
        ],
        compiler_params=pltpu.CompilerParams(collective_id=0, has_side_effects=True),
        name="gather_gram",
    )(pred, targ, var)


def rows_of(value, j):
    return jnp.broadcast_to(value[j : j + 1, :], value.shape)


def lanes_of(value, j):
    return jnp.broadcast_to(value[:, j : j + 1], value.shape)


def tree(parts):
    while len(parts) > 1:
        parts = [parts[i] + parts[i + 1] for i in range(0, len(parts), 2)]
    return parts[0]
def split(value):
    high = value.astype(BF16)
    rest = value - high.astype(F32)
    mid = rest.astype(BF16)
    return high, mid, (rest - mid.astype(F32)).astype(BF16)
def left_of(value):
    high, mid, low = split(value)
    return jnp.concatenate([high, high, mid, mid, high, low], axis=1)
def right_of(value):
    high, mid, low = split(value)
    return jnp.concatenate([high, mid, high, mid, low, high], axis=0)
def mm(left, right):
    return jnp.dot(left, right, preferred_element_type=F32)

def pivot_pair(j, cols, rows, sub):
    k = j + 1
    first, second = sub == j, sub == k
    pair = first | second
    a, b, c = rows_of(cols[j], j), rows_of(cols[k], j), rows_of(cols[k], k)
    ia = 1.0 / a
    isc = a * (1.0 / (a * c - b * b))
    cj = jnp.where(first, -1.0, jnp.where(second, 0.0, cols[j]))
    ck = jnp.where(second, -1.0, jnp.where(first, 0.0, cols[k])) - (cj * b) * ia
    bia, cja, cks = b * ia, cj * ia, ck * isc
    def reduce(t, soon):
        tj, tk = rows_of(t, j), rows_of(t, k)
        base = jnp.where(pair, 0.0, t)
        if soon:
            return base - (cj * tj) * ia - (ck * (tk - (b * tj) * ia)) * isc
        return base - cja * tj - cks * (tk - bia * tj)
    return [reduce(t, m <= k + 2) if m > k else t for m, t in enumerate(cols)], reduce(rows, False)

def sweep(groups, off, one):
    lane = lax.broadcasted_iota(jnp.int32, (8, TILE), 1)
    sub = lax.broadcasted_iota(jnp.int32, (8, TILE), 0)
    groups = list(groups)
    n = len(groups)
    for q in range(n):
        at = off + 8 * q
        here = (lane >= at) & (lane < at + 8)
        cols = [lanes_of(groups[q], at + j) * one for j in range(8)]
        rows = jnp.where(here, jnp.where(lane - at == sub, 1.0, 0.0), groups[q])
        for j in range(0, 8, 2):
            cols, rows = pivot_pair(j, cols, rows, sub)
        final = [rows_of(rows, j) for j in range(8)]
        for r in [(q + 1 + i) % n for i in range(n - 1)]:
            take = tree([lanes_of(groups[r], at + j) * final[j] for j in range(8)])
            groups[r] = jnp.where(here, 0.0, groups[r]) - take
        groups[q] = rows
    return groups

def invert(tile, one):
    size = tile.shape[0]
    lane = lax.broadcasted_iota(jnp.int32, tile.shape, 1)
    for off in range(0, size, STRIP):
        left = left_of(tile[:, off : off + STRIP])
        groups = sweep([tile[off + 8 * r : off + 8 * r + 8, :] for r in range(STRIP // 8)], off, one)
        strip = jnp.concatenate(groups, axis=0)
        right = right_of(strip)
        own = (lane >= off) & (lane < off + STRIP)
        rest = jnp.where(own, 0.0, tile) - mm(left, right)
        parts = [rest[:off], strip, rest[off + STRIP :]]
        tile = jnp.concatenate([p for p in parts if p.shape[0]], axis=0)
    return tile


def solve(gram, cross, one):
    members = gram.shape[0]
    row = lax.broadcasted_iota(jnp.int32, gram.shape, 0)
    col = lax.broadcasted_iota(jnp.int32, gram.shape, 1)
    whole = gram + jnp.where(row == col, members - 1.0, 0.0)
    n = members // TILE
    cut = lambda k: slice(k * TILE, (k + 1) * TILE)
    tiles = [[whole[cut(i), cut(j)] for j in range(n)] for i in range(n)]
    sides = [cross[cut(i), :] for i in range(n)]
    for k in range(n):
        inverse = left_of(invert(tiles[k][k], one))
        after = mm(inverse, right_of(jnp.concatenate(tiles[k][k + 1 :] + [sides[k]], axis=1)))
        right = right_of(after)
        for i in range(n):
            if i != k:
                update = mm(left_of(tiles[i][k]), right)
                for j in range(k + 1, n):
                    tiles[i][j] = tiles[i][j] - update[:, cut(j - k - 1)]
                sides[i] = sides[i] - update[:, (n - k - 1) * TILE :]
        for j in range(k + 1, n):
            tiles[k][j] = after[:, cut(j - k - 1)]
        sides[k] = after[:, (n - k - 1) * TILE :]
    return jnp.concatenate(sides, axis=0)


def step_kernel(
    per_step, ids, gram, cross, dev, res, var_row, pair, taper, ens, out, ones, gains, mixer, gain_sum
):
    members, data = dev.shape
    slots = ids.shape[0]
    blocks = pair.shape[0]
    width = data // slots

    @pl.when(pl.program_id(0) == 0)
    def _():
        pairs = pair[...]
        tapers = taper[...]
        spread = ROWS * slots
        lane = lax.broadcasted_iota(jnp.int32, (blocks, spread), 1)
        weight = jnp.zeros((blocks, spread), F32)
        for s in range(slots):
            hit = jnp.where(pairs == ids[s], tapers, 0.0)
            total = jnp.sum(hit, axis=1, keepdims=True)
            weight = jnp.where(lane // ROWS == s, total, weight)
        sub = lax.broadcasted_iota(jnp.int32, (ROWS, spread), 0)
        place = lax.broadcasted_iota(jnp.int32, (ROWS, spread), 1) % ROWS == sub
        for c in range(blocks):
            row = jnp.broadcast_to(weight[c : c + 1, :], (ROWS, spread))
            mixer[c * ROWS : (c + 1) * ROWS, :] = jnp.where(place, row, 0.0).astype(BF16)
        ones[...] = jnp.ones_like(ones)
        xt = jnp.transpose(solve(gram[...], cross[...], ones[...]))
        high = xt.astype(BF16)
        rest = xt - high.astype(F32)
        mid = rest.astype(BF16)
        low = (rest - mid.astype(F32)).astype(BF16)
        split = jnp.concatenate([high, mid, low], axis=0)
        for s in range(0, data, 2 * width):
            cols = slice(s, s + 2 * width)
            d = dev[:, cols]
            parts = jnp.dot(split, d, preferred_element_type=F32)
            update = parts[:members] + (parts[members : 2 * members] + parts[2 * members :])
            v = ((res[:, cols].astype(F32) - update) / var_row[:, cols]).astype(BF16)
            for k in range(2):
                half = slice(k * width, (k + 1) * width)
                gain = lax.dot_general(v[:, half], d[:, half], NT, preferred_element_type=F32)
                gains[s // width + k] = (gain * (1.0 / (members - 1.0))).astype(BF16)
        mix = mixer[...]
        for j in range(0, members, ROWS):
            stack = gains[:, j : j + ROWS, :].reshape(slots * ROWS, members)
            mixed = jnp.dot(mix, stack, preferred_element_type=F32).astype(BF16)
            gain_sum[:, j : j + ROWS, :] = mixed.reshape(blocks, ROWS, members)

    cell = ens.shape[1] // per_step
    for k in range(per_step):
        c = pl.program_id(0) * per_step + k
        u = ens[:, k * cell : (k + 1) * cell].astype(F32)
        u = (u - jnp.mean(u, axis=0, keepdims=True)).astype(BF16)
        out[:, k * cell : (k + 1) * cell] = jnp.dot(gain_sum[c], u, preferred_element_type=F32)


def finish(ensemble, gram, cross, dev, res, var_row, ids, pair, taper):
    members, cells = ensemble.shape
    blocks = pair.shape[0]
    slots = ids.shape[0]
    per_step = 4
    lanes = cells // blocks * per_step
    whole = lambda a: pl.BlockSpec(a.shape, lambda i: (0, 0), pipeline_mode=pl.Buffered(1))
    return pl.pallas_call(
        functools.partial(step_kernel, per_step),
        out_shape=jax.ShapeDtypeStruct((members, cells), F32),
        grid=(blocks // per_step,),
        in_specs=[pl.BlockSpec(memory_space=pltpu.SMEM)]
        + [whole(a) for a in (gram, cross, dev, res, var_row, pair, taper)]
        + [pl.BlockSpec((members, lanes), lambda i: (0, i))],
        out_specs=pl.BlockSpec((members, lanes), lambda i: (0, i)),
        scratch_shapes=[
            pltpu.VMEM((8, TILE), F32),
            pltpu.VMEM((slots, members, members), BF16),
            pltpu.VMEM((blocks * ROWS, slots * ROWS), BF16),
            pltpu.VMEM((blocks, members, members), BF16),
        ],
        name="solve_step",
    )(ids, gram, cross, dev, res, var_row, pair, taper, ensemble)


def solution(mesh):
    n = mesh.shape["blk"]

    def per_device(ensemble, predicted, targets, datum_noise_variance, block_ids, pair_blocks, taper):
        dev, res, var_row, gram, cross = gather(
            n, predicted, targets, datum_noise_variance.reshape(1, -1)
        )
        return finish(ensemble, gram, cross, dev, res, var_row, block_ids, pair_blocks, taper)

    in_specs = (
        P(None, ("groups", "blk")),
        P(None, ("groups", "blk")),
        P(None, ("groups", "blk")),
        P(("groups", "blk")),
        P("groups"),
        P(("groups", "blk"), None),
        P(("groups", "blk"), None),
    )
    return jax.shard_map(
        per_device, mesh=mesh, in_specs=in_specs, out_specs=P(None, ("groups", "blk")), check_vma=False
    )
```

```python
import functools

import jax
import jax.numpy as jnp
from jax import lax
from jax.experimental import pallas as pl
from jax.experimental.pallas import tpu as pltpu
from jax.sharding import PartitionSpec as P

MESH = pl.DeviceIdType.MESH
F32 = jnp.float32
BF16 = jnp.bfloat16
NT = (((1,), (1,)), ((), ()))
TILE = 128
EXTRA = 16
STRIP = 16
ROWS = 16


def chip_grid(n):
    chips = n // 2
    nx = max(f for f in range(1, chips + 1) if chips % f == 0 and f * f * f <= chips)
    return chips // nx, nx


def rows_of(value, j):
    return jnp.broadcast_to(value[j : j + 1, :], value.shape)


def lanes_of(value, j):
    return jnp.broadcast_to(value[:, j : j + 1], value.shape)


def tree(parts):
    while len(parts) > 1:
        parts = [parts[i] + parts[i + 1] for i in range(0, len(parts), 2)]
    return parts[0]
def split(value):
    high = value.astype(BF16)
    rest = value - high.astype(F32)
    mid = rest.astype(BF16)
    return high, mid, (rest - mid.astype(F32)).astype(BF16)
def left_of(value):
    high, mid, low = split(value)
    return jnp.concatenate([high, high, mid, mid, high, low], axis=1)
def right_of(value):
    high, mid, low = split(value)
    return jnp.concatenate([high, mid, high, mid, low, high], axis=0)
def mm(left, right):
    return jnp.dot(left, right, preferred_element_type=F32)

def pivot_pair(j, cols, rows, sub):
    k = j + 1
    first, second = sub == j, sub == k
    pair = first | second
    a, b, c = rows_of(cols[j], j), rows_of(cols[k], j), rows_of(cols[k], k)
    ia = 1.0 / a
    isc = a * (1.0 / (a * c - b * b))
    cj = jnp.where(first, -1.0, jnp.where(second, 0.0, cols[j]))
    ck = jnp.where(second, -1.0, jnp.where(first, 0.0, cols[k])) - (cj * b) * ia
    bia, cja, cks = b * ia, cj * ia, ck * isc
    def reduce(t, soon):
        tj, tk = rows_of(t, j), rows_of(t, k)
        base = jnp.where(pair, 0.0, t)
        if soon:
            return base - (cj * tj) * ia - (ck * (tk - (b * tj) * ia)) * isc
        return base - cja * tj - cks * (tk - bia * tj)
    return [reduce(t, m <= k + 2) if m > k else t for m, t in enumerate(cols)], reduce(rows, False)

def sweep(groups, off, one):
    lane = lax.broadcasted_iota(jnp.int32, (8, TILE), 1)
    sub = lax.broadcasted_iota(jnp.int32, (8, TILE), 0)
    groups = list(groups)
    n = len(groups)
    for q in range(n):
        at = off + 8 * q
        here = (lane >= at) & (lane < at + 8)
        cols = [lanes_of(groups[q], at + j) * one for j in range(8)]
        rows = jnp.where(here, jnp.where(lane - at == sub, 1.0, 0.0), groups[q])
        for j in range(0, 8, 2):
            cols, rows = pivot_pair(j, cols, rows, sub)
        final = [rows_of(rows, j) for j in range(8)]
        for r in [(q + 1 + i) % n for i in range(n - 1)]:
            take = tree([lanes_of(groups[r], at + j) * final[j] for j in range(8)])
            groups[r] = jnp.where(here, 0.0, groups[r]) - take
        groups[q] = rows
    return groups

def invert(tile, one, pause):
    size = tile.shape[0]
    lane = lax.broadcasted_iota(jnp.int32, tile.shape, 1)
    for off in range(0, size, STRIP):
        if off == size // 2:
            pause()
        left = left_of(tile[:, off : off + STRIP])
        groups = sweep([tile[off + 8 * r : off + 8 * r + 8, :] for r in range(STRIP // 8)], off, one)
        strip = jnp.concatenate(groups, axis=0)
        right = right_of(strip)
        own = (lane >= off) & (lane < off + STRIP)
        rest = jnp.where(own, 0.0, tile) - mm(left, right)
        parts = [rest[:off], strip, rest[off + STRIP :]]
        tile = jnp.concatenate([p for p in parts if p.shape[0]], axis=0)
    return tile


def invert_all(whole, one, pause):
    n = whole.shape[0] // TILE
    cut = lambda k: slice(k * TILE, (k + 1) * TILE)
    tiles = [[whole[cut(i), cut(j)] for j in range(n)] for i in range(n)]
    for k in range(n):
        others = [i for i in range(n) if i != k]
        inverse = invert(tiles[k][k], one, pause)
        pause()
        after = {j: mm(left_of(inverse), right_of(tiles[k][j])) for j in others}
        for i in others:
            left = left_of(tiles[i][k])
            for j in others:
                tiles[i][j] = tiles[i][j] - mm(left, right_of(after[j]))
            tiles[i][k] = -mm(left, right_of(inverse))
        for j in others:
            tiles[k][j] = after[j]
        tiles[k][k] = inverse
    return jnp.concatenate([jnp.concatenate(row, axis=1) for row in tiles], axis=0)


def gains_kernel(
    nz, nx, pred, targ, var, gains,
    dbuf, rbuf, sbuf, pbuf, tbuf, wbuf, total, ones,
    local_sem, zsend, xsend, csend, recv,
):
    members, width = pred.shape
    n = nz * nx * 2
    me = lax.axis_index("blk")
    core = me % 2
    x = (me // 2) % nx
    z = me // (2 * nx)
    place = lambda zo, xo, co: (zo * nx + xo) * 2 + co
    sibling = me + 1 - 2 * core

    local = (
        pltpu.make_async_copy(pred, pbuf, local_sem.at[0]),
        pltpu.make_async_copy(var, wbuf, local_sem.at[1]),
        pltpu.make_async_copy(targ, tbuf, local_sem.at[2]),
    )
    for copy in local:
        copy.start()
    ones[...] = jnp.ones_like(ones)
    total[...] = jnp.zeros_like(total)
    barrier = pltpu.get_barrier_semaphore()

    def greet(device):
        pl.semaphore_signal(barrier, inc=1, device_id={"blk": device}, device_id_type=MESH)

    for zo in range(nz):
        @pl.when(zo != z)
        def _(zo=zo):
            greet(place(zo, x, core))
    for xo in range(nx):
        @pl.when(xo != x)
        def _(xo=xo):
            greet(place(z, xo, core))
    greet(sibling)

    for copy in local[:2]:
        copy.wait()
    p = pbuf[...].astype(F32)
    db = (p - jnp.mean(p, axis=0, keepdims=True)).astype(BF16)
    parts = split(jnp.broadcast_to(wbuf[...], (EXTRA, width)))
    sub = lax.broadcasted_iota(jnp.int32, (EXTRA, width), 0)
    tail = jnp.where(sub == 0, parts[0].astype(F32), jnp.where(sub == 1, parts[1].astype(F32), parts[2].astype(F32)))
    dbuf[me, :members] = db
    dbuf[me, members:] = tail.astype(BF16)
    local[2].wait()
    rbuf[me] = (tbuf[...].astype(F32) - p).astype(BF16)
    pl.semaphore_wait(barrier, nz + nx - 1)

    bufs = (dbuf, rbuf)

    def send(h, o, sem, device):
        return pltpu.make_async_remote_copy(
            src_ref=bufs[h].at[o], dst_ref=bufs[h].at[o], send_sem=sem,
            recv_sem=recv.at[h, o], device_id={"blk": device}, device_id_type=MESH,
        )

    def z_copy(h, to):
        return send(h, me, zsend.at[h, to], place(to, x, core))

    def x_copy(h, zo, to):
        return send(h, place(zo, x, core), xsend.at[h, zo, to], place(z, to, core))

    def c_copy(h, o):
        return send(h, o, csend.at[h, o], sibling)

    def each_x(fn):
        for xo in range(nx):
            @pl.when(xo != x)
            def _(xo=xo):
                fn(xo)

    def each_z(fn):
        for d in range(nz - 1, 0, -1):
            for zo in (z - d, z + d):
                @pl.when((zo >= 0) & (zo < nz))
                def _(zo=zo):
                    fn(zo)

    for h in range(2):
        each_x(lambda xo: x_copy(h, z, xo).start())
        each_z(lambda zo: z_copy(h, zo).start())
        c_copy(h, me).start()

    def lagged(t, lag):
        d = t // 2 - lag
        s = 1 - 2 * (t % 2)
        zo = z - s * d
        valid = (d >= 0) & (zo >= 0) & (zo < nz) & ((d > 0) | (s == 1))
        return d, zo, valid

    def forward(h, t):
        d, zo, valid = lagged(t, 0)

        @pl.when(valid & (d > 0))
        def _():
            o = place(zo, x, core)
            c_copy(h, o).wait_recv()
            each_x(lambda xo: x_copy(h, zo, xo).start())
            c_copy(h, o).start()
        _, zx, valid_x = lagged(t, 1)

        @pl.when(valid_x)
        def _():
            def over(xo):
                o = place(zx, xo, core)
                c_copy(h, o).wait_recv()
                c_copy(h, o).start()
            each_x(over)

    def variance(o):
        tail = dbuf[o, members:].astype(F32)
        return tail[0:1] + tail[1:2] + tail[2:3]

    def absorb(o):
        db = dbuf[o, :members]
        sb = (db.astype(F32) * (1.0 / variance(o))).astype(BF16)
        sbuf[o] = sb
        total[...] += lax.dot_general(sb, db, NT, preferred_element_type=F32)

    def step(t, carry):
        forward(0, t)
        _, zo, valid = lagged(t, 0)

        @pl.when(valid)
        def _():
            absorb(place(zo, x, core))
        _, zx, valid_x = lagged(t, 1)

        @pl.when(valid_x)
        def _():
            each_x(lambda xo: absorb(place(zx, xo, core)))
            o = place(zx, x, 1 - core)
            c_copy(0, o).wait_recv()
            absorb(o)
        _, zp, valid_p = lagged(t, 2)

        @pl.when(valid_p)
        def _():
            def over(xo):
                o = place(zp, xo, 1 - core)
                c_copy(0, o).wait_recv()
                absorb(o)
            each_x(over)
        return carry

    lax.fori_loop(0, 2 * (nz + 2), step, 0)

    steps = 2 * (nz + 1)
    pauses = 2 * (members // TILE)
    count = [0]

    def pause():
        first = count[0] * steps // pauses
        count[0] += 1
        last = count[0] * steps // pauses
        lax.fori_loop(first, last, lambda t, carry: (forward(1, t), carry)[1], 0)

    row = lax.broadcasted_iota(jnp.int32, total.shape, 0)
    col = lax.broadcasted_iota(jnp.int32, total.shape, 1)
    whole = total[...] + jnp.where(row == col, members - 1.0, 0.0)
    inverse = right_of(invert_all(whole, ones[...], pause))

    def last(k, carry):
        c_copy(1, k * 2 + 1 - core).wait_recv()
        return carry

    lax.fori_loop(0, nz * nx, last, 0)

    group = 8

    def gather_cross(g, carry):
        left = jnp.concatenate([rbuf[g * group + i] for i in range(group)], axis=1)
        right = jnp.concatenate([sbuf[g * group + i] for i in range(group)], axis=1)
        product = lax.dot_general(left, right, NT, preferred_element_type=F32)
        total[...] = jnp.where(g == 0, product, total[...] + product)
        return carry

    lax.fori_loop(0, n // group, gather_cross, 0)
    xt = mm(left_of(total[...]), inverse)
    stack = jnp.concatenate(split(xt), axis=0)

    def finish(g, carry):
        for i in range(0, group, 2):
            o = g * group + i
            d = jnp.concatenate([dbuf[o, :members], dbuf[o + 1, :members]], axis=1)
            r = jnp.concatenate([rbuf[o], rbuf[o + 1]], axis=1).astype(F32)
            w = jnp.concatenate([variance(o), variance(o + 1)], axis=1)
            w = 1.0 / (w * (members - 1.0))
            parts = mm(stack, d)
            update = parts[:members] + (parts[members : 2 * members] + parts[2 * members :])
            v = ((r - update) * w).astype(BF16)
            for k in range(2):
                half = slice(k * width, (k + 1) * width)
                gain = lax.dot_general(v[:, half], d[:, half], NT, preferred_element_type=F32)
                gains[o + k] = gain.astype(BF16)
        return carry

    lax.fori_loop(0, n // group, finish, 0)

    def drain(h):
        each_z(lambda zo: z_copy(h, zo).wait_send())

        def over_z(zo, carry):
            each_x(lambda xo: x_copy(h, zo, xo).wait_send())
            return carry
        lax.fori_loop(0, nz, over_z, 0)

        def over(k, carry):
            c_copy(h, k * 2 + core).wait_send()
            return carry
        lax.fori_loop(0, nz * nx, over, 0)

    drain(0)
    drain(1)


def all_gains(n, pred, targ, var):
    nz, nx = chip_grid(n)
    members, width = pred.shape
    hbm = pl.BlockSpec(memory_space=pl.ANY)
    vmem = pl.BlockSpec(memory_space=pltpu.VMEM)
    sem = pltpu.SemaphoreType.DMA
    return pl.pallas_call(
        functools.partial(gains_kernel, nz, nx),
        out_shape=jax.ShapeDtypeStruct((n, members, members), BF16),
        in_specs=[hbm, hbm, hbm],
        out_specs=vmem,
        scratch_shapes=[
            pltpu.VMEM((n, members + EXTRA, width), BF16),
            pltpu.VMEM((n, members, width), BF16),
            pltpu.VMEM((n, members, width), BF16),
            pltpu.VMEM((members, width), BF16),
            pltpu.VMEM((members, width), BF16),
            pltpu.VMEM((1, width), F32),
            pltpu.VMEM((members, members), F32),
            pltpu.VMEM((8, TILE), F32),
            sem((3,)), sem((2, nz)), sem((2, nz, nx)), sem((2, n)), sem((2, n)),
        ],
        compiler_params=pltpu.CompilerParams(
            collective_id=0, has_side_effects=True, vmem_limit_bytes=48 << 20
        ),
        name="gather_gains",
    )(pred, targ, var)


def step_kernel(per_step, ids, gains, pair, taper, ens, out, mixer, gain_sum):
    slots, members, _ = gains.shape
    blocks = pair.shape[0]

    @pl.when(pl.program_id(0) == 0)
    def _():
        pairs = pair[...]
        tapers = taper[...]
        spread = ROWS * slots
        lane = lax.broadcasted_iota(jnp.int32, (blocks, spread), 1)
        weight = jnp.zeros((blocks, spread), F32)
        for s in range(slots):
            hit = jnp.where(pairs == ids[s], tapers, 0.0)
            both = jnp.sum(hit, axis=1, keepdims=True)
            weight = jnp.where(lane // ROWS == s, both, weight)
        sub = lax.broadcasted_iota(jnp.int32, (ROWS, spread), 0)
        spot = lax.broadcasted_iota(jnp.int32, (ROWS, spread), 1) % ROWS == sub
        for c in range(blocks):
            row = jnp.broadcast_to(weight[c : c + 1, :], (ROWS, spread))
            mixer[c * ROWS : (c + 1) * ROWS, :] = jnp.where(spot, row, 0.0).astype(BF16)
        mix = mixer[...]
        for j in range(0, members, ROWS):
            stack = gains[:, j : j + ROWS, :].reshape(slots * ROWS, members)
            mixed = jnp.dot(mix, stack, preferred_element_type=F32).astype(BF16)
            gain_sum[:, j : j + ROWS, :] = mixed.reshape(blocks, ROWS, members)

    cell = ens.shape[1] // per_step
    for k in range(per_step):
        c = pl.program_id(0) * per_step + k
        u = ens[:, k * cell : (k + 1) * cell].astype(F32)
        u = (u - jnp.mean(u, axis=0, keepdims=True)).astype(BF16)
        out[:, k * cell : (k + 1) * cell] = jnp.dot(gain_sum[c], u, preferred_element_type=F32)


def finish(ensemble, gains, ids, pair, taper):
    members, cells = ensemble.shape
    blocks = pair.shape[0]
    slots = ids.shape[0]
    per_step = 4
    lanes = cells // blocks * per_step
    whole = lambda a: pl.BlockSpec(a.shape, lambda i: (0,) * a.ndim, pipeline_mode=pl.Buffered(1))
    return pl.pallas_call(
        functools.partial(step_kernel, per_step),
        out_shape=jax.ShapeDtypeStruct((members, cells), F32),
        grid=(blocks // per_step,),
        in_specs=[pl.BlockSpec(memory_space=pltpu.SMEM)]
        + [whole(a) for a in (gains, pair, taper)]
        + [pl.BlockSpec((members, lanes), lambda i: (0, i))],
        out_specs=pl.BlockSpec((members, lanes), lambda i: (0, i)),
        scratch_shapes=[
            pltpu.VMEM((blocks * ROWS, slots * ROWS), BF16),
            pltpu.VMEM((blocks, members, members), BF16),
        ],
        compiler_params=pltpu.CompilerParams(vmem_limit_bytes=48 << 20),
        name="mix_step",
    )(ids, gains, pair, taper, ensemble)


def solution(mesh):
    n = mesh.shape["blk"]

    def per_device(ensemble, predicted, targets, datum_noise_variance, block_ids, pair_blocks, taper):
        gains = all_gains(n, predicted, targets, datum_noise_variance.reshape(1, -1))
        return finish(ensemble, gains, block_ids, pair_blocks, taper)

    in_specs = (
        P(None, ("groups", "blk")),
        P(None, ("groups", "blk")),
        P(None, ("groups", "blk")),
        P(("groups", "blk")),
        P("groups"),
        P(("groups", "blk"), None),
        P(("groups", "blk"), None),
    )
    return jax.shard_map(
        per_device, mesh=mesh, in_specs=in_specs, out_specs=P(None, ("groups", "blk")), check_vma=False
    )
```

```python
import functools

import jax
import jax.numpy as jnp
from jax import lax
from jax.experimental import pallas as pl
from jax.experimental.pallas import tpu as pltpu
from jax.sharding import PartitionSpec as P

MESH = pl.DeviceIdType.MESH
F32 = jnp.float32
BF16 = jnp.bfloat16
NT = (((1,), (1,)), ((), ()))
TILE = 128
EXTRA = 16
VMEM = 54 << 20
TOGETHER = 2
STRIP = 16
ROWS = 16


def chip_grid(n):
    chips = n // 2
    nx = max(f for f in range(1, chips + 1) if chips % f == 0 and f * f * f <= chips)
    return chips // nx, nx


def rows_of(value, j):
    return jnp.broadcast_to(value[j : j + 1, :], value.shape)


def lanes_of(value, j):
    return jnp.broadcast_to(value[:, j : j + 1], value.shape)


def tree(parts):
    while len(parts) > 1:
        parts = [parts[i] + parts[i + 1] for i in range(0, len(parts), 2)]
    return parts[0]
def split(value):
    high = value.astype(BF16)
    rest = value - high.astype(F32)
    mid = rest.astype(BF16)
    return high, mid, (rest - mid.astype(F32)).astype(BF16)
def left_of(value):
    high, mid, low = split(value)
    return jnp.concatenate([high, high, mid, mid, high, low], axis=1)
def right_of(value):
    high, mid, low = split(value)
    return jnp.concatenate([high, mid, high, mid, low, high], axis=0)
def mm(left, right):
    return jnp.dot(left, right, preferred_element_type=F32)

def pivot_pair(j, cols, rows, sub):
    k = j + 1
    first, second = sub == j, sub == k
    pair = first | second
    a, b, c = rows_of(cols[j], j), rows_of(cols[k], j), rows_of(cols[k], k)
    ia = 1.0 / a
    isc = a * (1.0 / (a * c - b * b))
    cj = jnp.where(first, -1.0, jnp.where(second, 0.0, cols[j]))
    ck = jnp.where(second, -1.0, jnp.where(first, 0.0, cols[k])) - (cj * b) * ia
    bia, cja, cks = b * ia, cj * ia, ck * isc
    def reduce(t, soon):
        tj, tk = rows_of(t, j), rows_of(t, k)
        base = jnp.where(pair, 0.0, t)
        if soon:
            return base - (cj * tj) * ia - (ck * (tk - (b * tj) * ia)) * isc
        return base - cja * tj - cks * (tk - bia * tj)
    return [reduce(t, m <= k + 2) if m > k else t for m, t in enumerate(cols)], reduce(rows, False)

def sweep(groups, off, one):
    lane = lax.broadcasted_iota(jnp.int32, (8, TILE), 1)
    sub = lax.broadcasted_iota(jnp.int32, (8, TILE), 0)
    groups = list(groups)
    n = len(groups)
    for q in range(n):
        at = off + 8 * q
        here = (lane >= at) & (lane < at + 8)
        cols = [lanes_of(groups[q], at + j) * one for j in range(8)]
        rows = jnp.where(here, jnp.where(lane - at == sub, 1.0, 0.0), groups[q])
        for j in range(0, 8, 2):
            cols, rows = pivot_pair(j, cols, rows, sub)
        final = [rows_of(rows, j) for j in range(8)]
        for r in [(q + 1 + i) % n for i in range(n - 1)]:
            take = tree([lanes_of(groups[r], at + j) * final[j] for j in range(8)])
            groups[r] = jnp.where(here, 0.0, groups[r]) - take
        groups[q] = rows
    return groups

def invert(tile, one, pause):
    size = tile.shape[0]
    lane = lax.broadcasted_iota(jnp.int32, tile.shape, 1)
    for off in range(0, size, STRIP):
        if off == size // 2:
            pause()
        left = left_of(tile[:, off : off + STRIP])
        groups = sweep([tile[off + 8 * r : off + 8 * r + 8, :] for r in range(STRIP // 8)], off, one)
        strip = jnp.concatenate(groups, axis=0)
        right = right_of(strip)
        own = (lane >= off) & (lane < off + STRIP)
        rest = jnp.where(own, 0.0, tile) - mm(left, right)
        parts = [rest[:off], strip, rest[off + STRIP :]]
        tile = jnp.concatenate([p for p in parts if p.shape[0]], axis=0)
    return tile


def invert_all(whole, one, pause):
    n = whole.shape[0] // TILE
    cut = lambda k: slice(k * TILE, (k + 1) * TILE)
    tiles = [[whole[cut(i), cut(j)] for j in range(n)] for i in range(n)]
    for k in range(n):
        others = [i for i in range(n) if i != k]
        inverse = invert(tiles[k][k], one, pause)
        pause()
        after = {j: mm(left_of(inverse), right_of(tiles[k][j])) for j in others}
        for i in others:
            left = left_of(tiles[i][k])
            for j in others:
                tiles[i][j] = tiles[i][j] - mm(left, right_of(after[j]))
            tiles[i][k] = -mm(left, right_of(inverse))
        for j in others:
            tiles[k][j] = after[j]
        tiles[k][k] = inverse
    return jnp.concatenate([jnp.concatenate(row, axis=1) for row in tiles], axis=0)


def gains_kernel(
    nz, nx, pred, targ, var, gains,
    dbuf, rbuf, sbuf, gbuf, pbuf, tbuf, wbuf, total, ones,
    local_sem, out_sem, zsend, xsend, csend, recv,
):
    members, width = pred.shape
    n = nz * nx * 2
    me = lax.axis_index("blk")
    core = me % 2
    x = (me // 2) % nx
    z = me // (2 * nx)
    place = lambda zo, xo, co: (zo * nx + xo) * 2 + co
    sibling = me + 1 - 2 * core

    local = (
        pltpu.make_async_copy(pred, pbuf, local_sem.at[0]),
        pltpu.make_async_copy(var, wbuf, local_sem.at[1]),
        pltpu.make_async_copy(targ, tbuf, local_sem.at[2]),
    )
    for copy in local:
        copy.start()
    ones[...] = jnp.ones_like(ones)
    total[...] = jnp.zeros_like(total)
    barrier = pltpu.get_barrier_semaphore()

    def greet(device):
        pl.semaphore_signal(barrier, inc=1, device_id={"blk": device}, device_id_type=MESH)

    for zo in range(nz):
        @pl.when(zo != z)
        def _(zo=zo):
            greet(place(zo, x, core))
    for xo in range(nx):
        @pl.when(xo != x)
        def _(xo=xo):
            greet(place(z, xo, core))
    greet(sibling)

    for copy in local:
        copy.wait()
    p = pbuf[...].astype(F32)
    db = (p - jnp.mean(p, axis=0, keepdims=True)).astype(BF16)
    dbuf[me, :members] = db
    parts = split(jnp.broadcast_to(wbuf[...], (EXTRA, width)))
    sub = lax.broadcasted_iota(jnp.int32, (EXTRA, width), 0)
    tail = jnp.where(sub == 0, parts[0].astype(F32), jnp.where(sub == 1, parts[1].astype(F32), parts[2].astype(F32)))
    dbuf[me, members:] = tail.astype(BF16)
    rbuf[me] = (tbuf[...].astype(F32) - p).astype(BF16)
    pl.semaphore_wait(barrier, nz + nx - 1)

    bufs = (dbuf, rbuf)

    def send(h, o, sem, device):
        return pltpu.make_async_remote_copy(
            src_ref=bufs[h].at[o], dst_ref=bufs[h].at[o], send_sem=sem,
            recv_sem=recv.at[h, o], device_id={"blk": device}, device_id_type=MESH,
        )

    def z_copy(h, to):
        return send(h, me, zsend.at[h, to], place(to, x, core))

    def x_copy(h, zo, to):
        return send(h, place(zo, x, core), xsend.at[h, zo, to], place(z, to, core))

    def c_copy(h, o):
        return send(h, o, csend.at[h, o], sibling)

    def each_x(fn):
        for xo in range(nx):
            @pl.when(xo != x)
            def _(xo=xo):
                fn(xo)

    def each_z(fn):
        for d in range(1, nz):
            for zo in (z - d, z + d):
                @pl.when((zo >= 0) & (zo < nz))
                def _(zo=zo):
                    fn(zo)

    def launch(h):
        each_x(lambda xo: x_copy(h, z, xo).start())
        each_z(lambda zo: z_copy(h, zo).start())
        c_copy(h, me).start()

    launch(0)

    def lagged(t, lag):
        d = t // 2 - lag
        s = 1 - 2 * (t % 2)
        zo = z - s * d
        valid = (d >= 0) & (zo >= 0) & (zo < nz) & ((d > 0) | (s == 1))
        return d, zo, valid

    def forward_z(h, t):
        d, zo, valid = lagged(t, 0)

        @pl.when(valid & (d > 0))
        def _():
            o = place(zo, x, core)
            c_copy(h, o).wait_recv()
            each_x(lambda xo: x_copy(h, zo, xo).start())
            c_copy(h, o).start()

    def forward_x(h, t, lag):
        _, zx, valid_x = lagged(t, lag)

        @pl.when(valid_x)
        def _():
            def over(xo):
                o = place(zx, xo, core)
                c_copy(h, o).wait_recv()
                c_copy(h, o).start()
            each_x(over)

    def variance(o):
        tail = dbuf[o, members:].astype(F32)
        return tail[0:1] + tail[1:2] + tail[2:3]

    def absorb(o):
        db = dbuf[o, :members]
        sb = (db.astype(F32) * (1.0 / variance(o))).astype(BF16)
        sbuf[o] = sb
        total[...] += lax.dot_general(sb, db, NT, preferred_element_type=F32)

    def step(t, carry):
        forward_z(0, t)

        @pl.when(t == 2 * nz - 1)
        def _():
            launch(1)

        forward_x(0, t, 1)
        _, zo, valid = lagged(t, 0)

        @pl.when(valid)
        def _():
            absorb(place(zo, x, core))
        _, zx, valid_x = lagged(t, 1)

        @pl.when(valid_x)
        def _():
            each_x(lambda xo: absorb(place(zx, xo, core)))
            o = place(zx, x, 1 - core)
            c_copy(0, o).wait_recv()
            absorb(o)
        _, zp, valid_p = lagged(t, 2)

        @pl.when(valid_p)
        def _():
            def over(xo):
                o = place(zp, xo, 1 - core)
                c_copy(0, o).wait_recv()
                absorb(o)
            each_x(over)
        return carry

    lax.fori_loop(0, 2 * (nz + 2), step, 0)

    pauses = 2 * (members // TILE)
    count = [0]

    def all_z(t, carry):
        forward_z(1, t)
        return carry

    def all_x(t, carry):
        forward_x(1, t, 0)
        return carry

    def pause():
        if count[0] == 1:
            lax.fori_loop(0, 2 * nz, all_z, 0)
        if count[0] == 3:
            lax.fori_loop(0, 2 * nz, all_x, 0)
        count[0] += 1

    row = lax.broadcasted_iota(jnp.int32, total.shape, 0)
    col = lax.broadcasted_iota(jnp.int32, total.shape, 1)
    whole = total[...] + jnp.where(row == col, members - 1.0, 0.0)
    pause()
    inverse = right_of(invert_all(whole, ones[...], pause))

    def last(k, carry):
        c_copy(1, k * 2 + 1 - core).wait_recv()
        return carry

    lax.fori_loop(0, nz * nx, last, 0)

    group = min(n, 16)

    def gather_cross(g, carry):
        left = jnp.concatenate([rbuf[g * group + i] for i in range(group)], axis=1)
        right = jnp.concatenate([sbuf[g * group + i] for i in range(group)], axis=1)
        product = lax.dot_general(left, right, NT, preferred_element_type=F32)
        total[...] = jnp.where(g == 0, product, total[...] + product)
        return carry

    lax.fori_loop(0, n // group, gather_cross, 0)
    xt = mm(left_of(total[...]), inverse)
    stack = jnp.concatenate(split(xt), axis=0)

    def innovate(g, carry):
        for i in range(0, group, 2):
            o = g * group + i
            d = jnp.concatenate([dbuf[o, :members], dbuf[o + 1, :members]], axis=1)
            r = jnp.concatenate([rbuf[o], rbuf[o + 1]], axis=1).astype(F32)
            w = jnp.concatenate([variance(o), variance(o + 1)], axis=1)
            w = 1.0 / (w * (members - 1.0))
            parts = mm(stack, d)
            update = parts[:members] + (parts[members : 2 * members] + parts[2 * members :])
            v = ((r - update) * w).astype(BF16)
            sbuf[o] = v[:, :width]
            sbuf[o + 1] = v[:, width:]
        return carry

    def out_copy(o):
        return pltpu.make_async_copy(gbuf.at[o], gains.at[o], out_sem.at[o])

    def gain(g, carry):
        for i in range(group):
            o = g * group + i
            product = lax.dot_general(sbuf[o], dbuf[o, :members], NT, preferred_element_type=F32)
            gbuf[o] = product.astype(BF16)
            out_copy(o).start()
        return carry

    lax.fori_loop(0, n // group, innovate, 0)
    lax.fori_loop(0, n // group, gain, 0)

    def drain(h):
        each_z(lambda zo: z_copy(h, zo).wait_send())

        def over_z(zo, carry):
            each_x(lambda xo: x_copy(h, zo, xo).wait_send())
            return carry
        lax.fori_loop(0, nz, over_z, 0)

        def over(k, carry):
            c_copy(h, k * 2 + core).wait_send()
            return carry
        lax.fori_loop(0, nz * nx, over, 0)

    drain(0)
    drain(1)

    def stored(o, carry):
        out_copy(o).wait()
        return carry

    lax.fori_loop(0, n, stored, 0)


def all_gains(n, pred, targ, var):
    nz, nx = chip_grid(n)
    members, width = pred.shape
    hbm = pl.BlockSpec(memory_space=pltpu.HBM)
    sem = pltpu.SemaphoreType.DMA
    return pl.pallas_call(
        functools.partial(gains_kernel, nz, nx),
        out_shape=jax.ShapeDtypeStruct((n, members, members), BF16),
        in_specs=[hbm, hbm, hbm],
        out_specs=hbm,
        scratch_shapes=[
            pltpu.VMEM((n, members + EXTRA, width), BF16),
            pltpu.VMEM((n, members, width), BF16),
            pltpu.VMEM((n, members, width), BF16),
            pltpu.VMEM((n, members, members), BF16),
            pltpu.VMEM((members, width), BF16),
            pltpu.VMEM((members, width), BF16),
            pltpu.VMEM((1, width), F32),
            pltpu.VMEM((members, members), F32),
            pltpu.VMEM((8, TILE), F32),
            sem((3,)), sem((n,)), sem((2, nz)), sem((2, nz, nx)), sem((2, n)), sem((2, n)),
        ],
        compiler_params=pltpu.CompilerParams(
            collective_id=0, has_side_effects=True, vmem_limit_bytes=VMEM
        ),
        name="gather_gains",
    )(pred, targ, var)


def step_kernel(
    ids, gains, pair, taper, ens, out,
    mixer, gain_sum, result, sems,
):
    slots, members, _ = gains.shape
    blocks = pair.shape[0]
    cell = ens.shape[1] // blocks
    pairs = pair[...]
    tapers = taper[...]
    spread = ROWS * slots
    lane = lax.broadcasted_iota(jnp.int32, (blocks, spread), 1)
    weight = jnp.zeros((blocks, spread), F32)
    for s in range(slots):
        hit = jnp.where(pairs == ids[s], tapers, 0.0)
        both = jnp.sum(hit, axis=1, keepdims=True)
        weight = jnp.where(lane // ROWS == s, both, weight)
    sub = lax.broadcasted_iota(jnp.int32, (ROWS, spread), 0)
    spot = lax.broadcasted_iota(jnp.int32, (ROWS, spread), 1) % ROWS == sub
    for c in range(blocks):
        row = jnp.broadcast_to(weight[c : c + 1, :], (ROWS, spread))
        mixer[c * ROWS : (c + 1) * ROWS, :] = jnp.where(spot, row, 0.0).astype(BF16)
    mix = mixer[...]
    strips = members // ROWS
    means = []
    for c in range(blocks):
        means.append(jnp.mean(ens[:, c * cell : (c + 1) * cell].astype(F32), axis=0, keepdims=True))
    for i in range(strips):
        rows = slice(i * ROWS, (i + 1) * ROWS)
        stack = gains[:, rows, :].reshape(slots * ROWS, members)
        mixed = jnp.dot(mix, stack, preferred_element_type=F32).astype(BF16)
        gain_sum[:, rows, :] = mixed.reshape(blocks, ROWS, members)
    copies = []
    for first in range(0, blocks, TOGETHER):
        for c in range(first, first + TOGETHER):
            cols = slice(c * cell, (c + 1) * cell)
            u = (ens[:, cols].astype(F32) - means[c]).astype(BF16)
            result[:, cols] = jnp.dot(gain_sum[c], u, preferred_element_type=F32)
        cols = pl.ds(first * cell, TOGETHER * cell)
        copies.append(pltpu.make_async_copy(result.at[:, cols], out.at[:, cols], sems.at[len(copies)]))
        copies[-1].start()
    for copy in copies:
        copy.wait()


def finish(ensemble, gains, ids, pair, taper):
    members, cells = ensemble.shape
    blocks = pair.shape[0]
    slots = ids.shape[0]
    hbm = pl.BlockSpec(memory_space=pltpu.HBM)
    vmem = pl.BlockSpec(memory_space=pltpu.VMEM)
    return pl.pallas_call(
        step_kernel,
        out_shape=jax.ShapeDtypeStruct((members, cells), F32),
        in_specs=[pl.BlockSpec(memory_space=pltpu.SMEM), vmem, vmem, vmem, vmem],
        out_specs=hbm,
        scratch_shapes=[
            pltpu.VMEM((blocks * ROWS, slots * ROWS), BF16),
            pltpu.VMEM((blocks, members, members), BF16),
            pltpu.VMEM((members, cells), F32),
            pltpu.SemaphoreType.DMA((blocks // TOGETHER,)),
        ],
        compiler_params=pltpu.CompilerParams(vmem_limit_bytes=48 << 20),
        name="mix_step",
    )(ids, gains, pair, taper, ensemble)


def solution(mesh):
    n = mesh.shape["blk"]

    def per_device(ensemble, predicted, targets, datum_noise_variance, block_ids, pair_blocks, taper):
        gains = all_gains(n, predicted, targets, datum_noise_variance.reshape(1, -1))
        return finish(ensemble, gains, block_ids, pair_blocks, taper)

    in_specs = (
        P(None, ("groups", "blk")),
        P(None, ("groups", "blk")),
        P(None, ("groups", "blk")),
        P(("groups", "blk")),
        P("groups"),
        P(("groups", "blk"), None),
        P(("groups", "blk"), None),
    )
    return jax.shard_map(
        per_device, mesh=mesh, in_specs=in_specs, out_specs=P(None, ("groups", "blk")), check_vma=False
    )
```

```python
import functools

import jax
import jax.numpy as jnp
from jax import lax
from jax.experimental import pallas as pl
from jax.experimental.pallas import tpu as pltpu
from jax.sharding import PartitionSpec as P

MESH = pl.DeviceIdType.MESH
F32 = jnp.float32
BF16 = jnp.bfloat16
NT = (((1,), (1,)), ((), ()))
TILE = 128
EXTRA = 16
SPARE = 64
PIECES = 2
PACE = 32
Z_SPOTS = (0, 4)
X_SPOTS = (3, 7)
VMEM = 54 << 20
TOGETHER = 2
STRIP = 16
ROWS = 16


def chip_grid(n):
    chips = n // 2
    nx = max(f for f in range(1, chips + 1) if chips % f == 0 and f * f * f <= chips)
    return chips // nx, nx


def rows_of(value, j):
    return jnp.broadcast_to(value[j : j + 1, :], value.shape)


def lanes_of(value, j):
    return jnp.broadcast_to(value[:, j : j + 1], value.shape)


def tree(parts):
    while len(parts) > 1:
        parts = [parts[i] + parts[i + 1] for i in range(0, len(parts), 2)]
    return parts[0]
def split(value):
    high = value.astype(BF16)
    rest = value - high.astype(F32)
    mid = rest.astype(BF16)
    return high, mid, (rest - mid.astype(F32)).astype(BF16)
def left_of(value):
    high, mid, low = split(value)
    return jnp.concatenate([high, high, mid, mid, high, low], axis=1)
def right_of(value):
    high, mid, low = split(value)
    return jnp.concatenate([high, mid, high, mid, low, high], axis=0)
def mm(left, right):
    return jnp.dot(left, right, preferred_element_type=F32)

def pivot_pair(j, cols, rows, sub):
    k = j + 1
    first, second = sub == j, sub == k
    pair = first | second
    a, b, c = rows_of(cols[j], j), rows_of(cols[k], j), rows_of(cols[k], k)
    ia = 1.0 / a
    isc = a * (1.0 / (a * c - b * b))
    cj = jnp.where(first, -1.0, jnp.where(second, 0.0, cols[j]))
    ck = jnp.where(second, -1.0, jnp.where(first, 0.0, cols[k])) - (cj * b) * ia
    bia, cja, cks = b * ia, cj * ia, ck * isc
    def reduce(t, soon):
        tj, tk = rows_of(t, j), rows_of(t, k)
        base = jnp.where(pair, 0.0, t)
        if soon:
            return base - (cj * tj) * ia - (ck * (tk - (b * tj) * ia)) * isc
        return base - cja * tj - cks * (tk - bia * tj)
    return [reduce(t, m <= k + 2) if m > k else t for m, t in enumerate(cols)], reduce(rows, False)

def sweep(groups, off, one):
    lane = lax.broadcasted_iota(jnp.int32, (8, TILE), 1)
    sub = lax.broadcasted_iota(jnp.int32, (8, TILE), 0)
    groups = list(groups)
    n = len(groups)
    for q in range(n):
        at = off + 8 * q
        here = (lane >= at) & (lane < at + 8)
        cols = [lanes_of(groups[q], at + j) * one for j in range(8)]
        rows = jnp.where(here, jnp.where(lane - at == sub, 1.0, 0.0), groups[q])
        for j in range(0, 8, 2):
            cols, rows = pivot_pair(j, cols, rows, sub)
        final = [rows_of(rows, j) for j in range(8)]
        for r in [(q + 1 + i) % n for i in range(n - 1)]:
            take = tree([lanes_of(groups[r], at + j) * final[j] for j in range(8)])
            groups[r] = jnp.where(here, 0.0, groups[r]) - take
        groups[q] = rows
    return groups

def invert(tile, one, pause):
    size = tile.shape[0]
    lane = lax.broadcasted_iota(jnp.int32, tile.shape, 1)
    for off in range(0, size, STRIP):
        if off and off % PACE == 0:
            pause()
        left = left_of(tile[:, off : off + STRIP])
        groups = sweep([tile[off + 8 * r : off + 8 * r + 8, :] for r in range(STRIP // 8)], off, one)
        strip = jnp.concatenate(groups, axis=0)
        right = right_of(strip)
        own = (lane >= off) & (lane < off + STRIP)
        rest = jnp.where(own, 0.0, tile) - mm(left, right)
        parts = [rest[:off], strip, rest[off + STRIP :]]
        tile = jnp.concatenate([p for p in parts if p.shape[0]], axis=0)
    return tile


def invert_all(whole, one, pause):
    n = whole.shape[0] // TILE
    cut = lambda k: slice(k * TILE, (k + 1) * TILE)
    tiles = [[whole[cut(i), cut(j)] for j in range(n)] for i in range(n)]
    for k in range(n):
        others = [i for i in range(n) if i != k]
        inverse = invert(tiles[k][k], one, pause)
        pause()
        after = {j: mm(left_of(inverse), right_of(tiles[k][j])) for j in others}
        for i in others:
            left = left_of(tiles[i][k])
            for j in others:
                tiles[i][j] = tiles[i][j] - mm(left, right_of(after[j]))
            tiles[i][k] = -mm(left, right_of(inverse))
        for j in others:
            tiles[k][j] = after[j]
        tiles[k][k] = inverse
    return jnp.concatenate([jnp.concatenate(row, axis=1) for row in tiles], axis=0)


def gains_kernel(
    nz, nx, pred, targ, var, gains,
    dbuf, rbuf, sbuf, gbuf, pbuf, tbuf, wbuf, total, ones,
    local_sem, out_sem, zsend, xsend, csend, recv,
):
    members, width = pred.shape
    n = nz * nx * 2
    me = lax.axis_index("blk")
    core = me % 2
    x = (me // 2) % nx
    z = me // (2 * nx)
    place = lambda zo, xo, co: (zo * nx + xo) * 2 + co
    sibling = me + 1 - 2 * core

    local = (
        pltpu.make_async_copy(pred, pbuf, local_sem.at[0]),
        pltpu.make_async_copy(var, wbuf, local_sem.at[1]),
        pltpu.make_async_copy(targ, tbuf, local_sem.at[2]),
    )
    for copy in local:
        copy.start()
    ones[...] = jnp.ones_like(ones)
    total[...] = jnp.zeros_like(total)
    barrier = pltpu.get_barrier_semaphore()

    def greet(device):
        pl.semaphore_signal(barrier, inc=1, device_id={"blk": device}, device_id_type=MESH)

    for zo in range(nz):
        @pl.when(zo != z)
        def _(zo=zo):
            greet(place(zo, x, core))
    for xo in range(nx):
        @pl.when(xo != x)
        def _(xo=xo):
            greet(place(z, xo, core))
    greet(sibling)

    for copy in local:
        copy.wait()
    p = pbuf[...].astype(F32)
    db = (p - jnp.mean(p, axis=0, keepdims=True)).astype(BF16)
    dbuf[me, :members] = db
    parts = split(jnp.broadcast_to(wbuf[...], (EXTRA, width)))
    sub = lax.broadcasted_iota(jnp.int32, (EXTRA, width), 0)
    tail = jnp.where(sub == 0, parts[0].astype(F32), jnp.where(sub == 1, parts[1].astype(F32), parts[2].astype(F32)))
    dbuf[me, members:] = tail.astype(BF16)
    rbuf[me] = (tbuf[...].astype(F32) - p).astype(BF16)
    pl.semaphore_wait(barrier, nz + nx - 1)

    bufs = (dbuf, rbuf)

    def send(h, o, sem, device):
        return pltpu.make_async_remote_copy(
            src_ref=bufs[h].at[o], dst_ref=bufs[h].at[o], send_sem=sem,
            recv_sem=recv.at[h, o], device_id={"blk": device}, device_id_type=MESH,
        )

    def z_copy(h, to):
        return send(h, me, zsend.at[h, to], place(to, x, core))

    def x_copy(h, zo, to):
        return send(h, place(zo, x, core), xsend.at[h, zo, to], place(z, to, core))

    def c_copy(h, o):
        return send(h, o, csend.at[h, o], sibling)

    def each_x(fn):
        for xo in range(nx):
            @pl.when(xo != x)
            def _(xo=xo):
                fn(xo)

    def each_z(fn):
        for d in range(1, nz):
            for zo in (z - d, z + d):
                @pl.when((zo >= 0) & (zo < nz))
                def _(zo=zo):
                    fn(zo)

    def launch(h):
        each_x(lambda xo: x_copy(h, z, xo).start())
        each_z(lambda zo: z_copy(h, zo).start())
        c_copy(h, me).start()

    launch(0)

    def lagged(t, lag):
        d = t // 2 - lag
        s = 1 - 2 * (t % 2)
        zo = z - s * d
        valid = (d >= 0) & (zo >= 0) & (zo < nz) & ((d > 0) | (s == 1))
        return d, zo, valid

    def forward_z(h, t):
        d, zo, valid = lagged(t, 0)

        @pl.when(valid & (d > 0))
        def _():
            o = place(zo, x, core)
            c_copy(h, o).wait_recv()
            each_x(lambda xo: x_copy(h, zo, xo).start())
            c_copy(h, o).start()

    def forward_x(h, t, lag):
        _, zx, valid_x = lagged(t, lag)

        @pl.when(valid_x)
        def _():
            def over(xo):
                o = place(zx, xo, core)
                c_copy(h, o).wait_recv()
                c_copy(h, o).start()
            each_x(over)

    def variance(o):
        tail = dbuf[o, members:].astype(F32)
        return tail[0:1] + tail[1:2] + tail[2:3]

    def absorb(o):
        db = dbuf[o, :members]
        sb = (db.astype(F32) * (1.0 / variance(o))).astype(BF16)
        sbuf[o] = sb
        total[...] += lax.dot_general(sb, db, NT, preferred_element_type=F32)

    def step(t, carry):
        forward_z(0, t)

        @pl.when(t == 2 * nz - 1)
        def _():
            launch(1)

        forward_x(0, t, 1)
        _, zo, valid = lagged(t, 0)

        @pl.when(valid)
        def _():
            absorb(place(zo, x, core))
        _, zx, valid_x = lagged(t, 1)

        @pl.when(valid_x)
        def _():
            each_x(lambda xo: absorb(place(zx, xo, core)))
            o = place(zx, x, 1 - core)
            c_copy(0, o).wait_recv()
            absorb(o)
        _, zp, valid_p = lagged(t, 2)

        @pl.when(valid_p)
        def _():
            def over(xo):
                o = place(zp, xo, 1 - core)
                c_copy(0, o).wait_recv()
                absorb(o)
            each_x(over)
        return carry

    lax.fori_loop(0, 2 * (nz + 2), step, 0)

    count = [0]

    def relay(fn, spots):
        first, last = spots

        def one(t, carry):
            fn(t)
            return carry

        for d in range(nz):
            spot = first + (last - first) * d // (nz - 1)
            if spot == count[0]:
                lax.fori_loop(2 * d, 2 * d + 2, one, 0)

    def pause():
        relay(lambda t: forward_z(1, t), Z_SPOTS)
        relay(lambda t: forward_x(1, t, 0), X_SPOTS)
        count[0] += 1

    row = lax.broadcasted_iota(jnp.int32, total.shape, 0)
    col = lax.broadcasted_iota(jnp.int32, total.shape, 1)
    whole = total[...] + jnp.where(row == col, members - 1.0, 0.0)
    pause()
    inverse = right_of(invert_all(whole, ones[...], pause))

    def last(k, carry):
        c_copy(1, k * 2 + 1 - core).wait_recv()
        return carry

    lax.fori_loop(0, nz * nx, last, 0)

    group = min(n, 16)

    def gather_cross(g, carry):
        left = jnp.concatenate([rbuf[g * group + i] for i in range(group)], axis=1)
        right = jnp.concatenate([sbuf[g * group + i] for i in range(group)], axis=1)
        product = lax.dot_general(left, right, NT, preferred_element_type=F32)
        total[...] = jnp.where(g == 0, product, total[...] + product)
        return carry

    lax.fori_loop(0, n // group, gather_cross, 0)
    xt = mm(left_of(total[...]), inverse)
    stack = jnp.concatenate(split(xt), axis=0)

    def innovate(g, carry):
        for i in range(0, group, 2):
            o = g * group + i
            d = jnp.concatenate([dbuf[o, :members], dbuf[o + 1, :members]], axis=1)
            r = jnp.concatenate([rbuf[o], rbuf[o + 1]], axis=1).astype(F32)
            w = jnp.concatenate([variance(o), variance(o + 1)], axis=1)
            w = 1.0 / (w * (members - 1.0))
            parts = mm(stack, d)
            update = parts[:members] + (parts[members : 2 * members] + parts[2 * members :])
            v = ((r - update) * w).astype(BF16)
            sbuf[o] = v[:, :width]
            sbuf[o + 1] = v[:, width:]
        return carry

    def out_copy(o):
        return pltpu.make_async_copy(gbuf.at[o], gains.at[o], out_sem.at[o])

    def gain(g, carry):
        for i in range(group):
            o = g * group + i
            product = lax.dot_general(sbuf[o], dbuf[o, :members], NT, preferred_element_type=F32)
            gbuf[o] = product.astype(BF16)
            out_copy(o).start()
        return carry

    lax.fori_loop(0, n // group, innovate, 0)
    lax.fori_loop(0, n // group, gain, 0)

    def drain(h):
        each_z(lambda zo: z_copy(h, zo).wait_send())

        def over_z(zo, carry):
            each_x(lambda xo: x_copy(h, zo, xo).wait_send())
            return carry
        lax.fori_loop(0, nz, over_z, 0)

        def over(k, carry):
            c_copy(h, k * 2 + core).wait_send()
            return carry
        lax.fori_loop(0, nz * nx, over, 0)

    drain(0)
    drain(1)

    def stored(o, carry):
        out_copy(o).wait()
        return carry

    lax.fori_loop(0, n, stored, 0)


def all_gains(n, pred, targ, var):
    nz, nx = chip_grid(n)
    members, width = pred.shape
    hbm = pl.BlockSpec(memory_space=pltpu.HBM)
    sem = pltpu.SemaphoreType.DMA
    return pl.pallas_call(
        functools.partial(gains_kernel, nz, nx),
        out_shape=jax.ShapeDtypeStruct((n + SPARE, members, members), BF16),
        in_specs=[hbm, hbm, hbm],
        out_specs=hbm,
        scratch_shapes=[
            pltpu.VMEM((n, members + EXTRA, width), BF16),
            pltpu.VMEM((n, members, width), BF16),
            pltpu.VMEM((n, members, width), BF16),
            pltpu.VMEM((n, members, members), BF16),
            pltpu.VMEM((members, width), BF16),
            pltpu.VMEM((members, width), BF16),
            pltpu.VMEM((1, width), F32),
            pltpu.VMEM((members, members), F32),
            pltpu.VMEM((8, TILE), F32),
            sem((3,)), sem((n,)), sem((2, nz)), sem((2, nz, nx)), sem((2, n)), sem((2, n)),
        ],
        compiler_params=pltpu.CompilerParams(
            collective_id=0, has_side_effects=True, vmem_limit_bytes=VMEM
        ),
        name="gather_gains",
    )(pred, targ, var)


def step_kernel(
    ids, far_gains, pair, taper, ens, out,
    gains, mixer, gain_sum, result, gain_sem, sems,
):
    slots, members, _ = gains.shape
    blocks = pair.shape[0]
    cell = ens.shape[1] // blocks
    piece = members // PIECES
    gain_copies = []
    for k in range(PIECES):
        some = pl.ds(k * piece, piece)
        gain_copies.append(
            pltpu.make_async_copy(far_gains.at[pl.ds(0, slots), some], gains.at[:, some], gain_sem.at[k])
        )
        gain_copies[-1].start()
    pairs = pair[...]
    tapers = taper[...]
    spread = ROWS * slots
    lane = lax.broadcasted_iota(jnp.int32, (blocks, spread), 1)
    weight = jnp.zeros((blocks, spread), F32)
    for s in range(slots):
        hit = jnp.where(pairs == ids[s], tapers, 0.0)
        both = jnp.sum(hit, axis=1, keepdims=True)
        weight = jnp.where(lane // ROWS == s, both, weight)
    sub = lax.broadcasted_iota(jnp.int32, (ROWS, spread), 0)
    spot = lax.broadcasted_iota(jnp.int32, (ROWS, spread), 1) % ROWS == sub
    for c in range(blocks):
        row = jnp.broadcast_to(weight[c : c + 1, :], (ROWS, spread))
        mixer[c * ROWS : (c + 1) * ROWS, :] = jnp.where(spot, row, 0.0).astype(BF16)
    mix = mixer[...]
    strips = members // ROWS
    means = []
    for c in range(blocks):
        means.append(jnp.mean(ens[:, c * cell : (c + 1) * cell].astype(F32), axis=0, keepdims=True))
    for i in range(strips):
        if i * ROWS % piece == 0:
            gain_copies[i * ROWS // piece].wait()
        rows = slice(i * ROWS, (i + 1) * ROWS)
        stack = gains[:, rows, :].reshape(slots * ROWS, members)
        mixed = jnp.dot(mix, stack, preferred_element_type=F32).astype(BF16)
        gain_sum[:, rows, :] = mixed.reshape(blocks, ROWS, members)
    copies = []
    for first in range(0, blocks, TOGETHER):
        for c in range(first, first + TOGETHER):
            cols = slice(c * cell, (c + 1) * cell)
            u = (ens[:, cols].astype(F32) - means[c]).astype(BF16)
            result[:, cols] = jnp.dot(gain_sum[c], u, preferred_element_type=F32)
        cols = pl.ds(first * cell, TOGETHER * cell)
        copies.append(pltpu.make_async_copy(result.at[:, cols], out.at[:, cols], sems.at[len(copies)]))
        copies[-1].start()
    for copy in copies:
        copy.wait()


def finish(ensemble, gains, ids, pair, taper):
    members, cells = ensemble.shape
    blocks = pair.shape[0]
    slots = ids.shape[0]
    hbm = pl.BlockSpec(memory_space=pltpu.HBM)
    vmem = pl.BlockSpec(memory_space=pltpu.VMEM)
    return pl.pallas_call(
        step_kernel,
        out_shape=jax.ShapeDtypeStruct((members, cells), F32),
        in_specs=[pl.BlockSpec(memory_space=pltpu.SMEM), hbm, vmem, vmem, vmem],
        out_specs=hbm,
        scratch_shapes=[
            pltpu.VMEM((slots, members, members), BF16),
            pltpu.VMEM((blocks * ROWS, slots * ROWS), BF16),
            pltpu.VMEM((blocks, members, members), BF16),
            pltpu.VMEM((members, cells), F32),
            pltpu.SemaphoreType.DMA((PIECES,)),
            pltpu.SemaphoreType.DMA((blocks // TOGETHER,)),
        ],
        compiler_params=pltpu.CompilerParams(vmem_limit_bytes=48 << 20),
        name="mix_step",
    )(ids, gains, pair, taper, ensemble)


def solution(mesh):
    n = mesh.shape["blk"]

    def per_device(ensemble, predicted, targets, datum_noise_variance, block_ids, pair_blocks, taper):
        gains = all_gains(n, predicted, targets, datum_noise_variance.reshape(1, -1))
        return finish(ensemble, gains, block_ids, pair_blocks, taper)

    in_specs = (
        P(None, ("groups", "blk")),
        P(None, ("groups", "blk")),
        P(None, ("groups", "blk")),
        P(("groups", "blk")),
        P("groups"),
        P(("groups", "blk"), None),
        P(("groups", "blk"), None),
    )
    return jax.shard_map(
        per_device, mesh=mesh, in_specs=in_specs, out_specs=P(None, ("groups", "blk")), check_vma=False
    )
```

```python
import functools

import jax
import jax.numpy as jnp
from jax import lax
from jax.experimental import pallas as pl
from jax.experimental.pallas import tpu as pltpu
from jax.sharding import PartitionSpec as P

MESH = pl.DeviceIdType.MESH
F32 = jnp.float32
BF16 = jnp.bfloat16
NT = (((1,), (1,)), ((), ()))
TILE = 128
EXTRA = 16
SPARE = 64
PIECES = 2
PACE = 32
Z_SPOTS = (0, 2)
X_SPOTS = (3, 6)
VMEM = 54 << 20
TOGETHER = 2
STRIP = 16
ROWS = 16


def chip_grid(n):
    chips = n // 2
    nx = max(f for f in range(1, chips + 1) if chips % f == 0 and f * f * f <= chips)
    return chips // nx, nx


def rows_of(value, j):
    return jnp.broadcast_to(value[j : j + 1, :], value.shape)


def lanes_of(value, j):
    return jnp.broadcast_to(value[:, j : j + 1], value.shape)


def tree(parts):
    while len(parts) > 1:
        parts = [parts[i] + parts[i + 1] for i in range(0, len(parts), 2)]
    return parts[0]
def split(value):
    high = value.astype(BF16)
    rest = value - high.astype(F32)
    mid = rest.astype(BF16)
    return high, mid, (rest - mid.astype(F32)).astype(BF16)
def left_of(value):
    high, mid, low = split(value)
    return jnp.concatenate([high, high, mid, mid, high, low], axis=1)
def right_of(value):
    high, mid, low = split(value)
    return jnp.concatenate([high, mid, high, mid, low, high], axis=0)
def mm(left, right):
    return jnp.dot(left, right, preferred_element_type=F32)

def pivot_pair(j, cols, rows, sub):
    k = j + 1
    first, second = sub == j, sub == k
    pair = first | second
    a, b, c = rows_of(cols[j], j), rows_of(cols[k], j), rows_of(cols[k], k)
    ia = 1.0 / a
    isc = a * (1.0 / (a * c - b * b))
    cj = jnp.where(first, -1.0, jnp.where(second, 0.0, cols[j]))
    ck = jnp.where(second, -1.0, jnp.where(first, 0.0, cols[k])) - (cj * b) * ia
    bia, cja, cks = b * ia, cj * ia, ck * isc
    def reduce(t, soon):
        tj, tk = rows_of(t, j), rows_of(t, k)
        base = jnp.where(pair, 0.0, t)
        if soon:
            return base - (cj * tj) * ia - (ck * (tk - (b * tj) * ia)) * isc
        return base - cja * tj - cks * (tk - bia * tj)
    return [reduce(t, m <= k + 2) if m > k else t for m, t in enumerate(cols)], reduce(rows, False)

def sweep(groups, off, one):
    lane = lax.broadcasted_iota(jnp.int32, (8, TILE), 1)
    sub = lax.broadcasted_iota(jnp.int32, (8, TILE), 0)
    groups = list(groups)
    n = len(groups)
    for q in range(n):
        at = off + 8 * q
        here = (lane >= at) & (lane < at + 8)
        cols = [lanes_of(groups[q], at + j) * one for j in range(8)]
        rows = jnp.where(here, jnp.where(lane - at == sub, 1.0, 0.0), groups[q])
        for j in range(0, 8, 2):
            cols, rows = pivot_pair(j, cols, rows, sub)
        final = [rows_of(rows, j) for j in range(8)]
        for r in [(q + 1 + i) % n for i in range(n - 1)]:
            take = tree([lanes_of(groups[r], at + j) * final[j] for j in range(8)])
            groups[r] = jnp.where(here, 0.0, groups[r]) - take
        groups[q] = rows
    return groups

def invert(tile, one, pause):
    size = tile.shape[0]
    lane = lax.broadcasted_iota(jnp.int32, tile.shape, 1)
    for off in range(0, size, STRIP):
        if off and off % PACE == 0:
            pause()
        left = left_of(tile[:, off : off + STRIP])
        groups = sweep([tile[off + 8 * r : off + 8 * r + 8, :] for r in range(STRIP // 8)], off, one)
        strip = jnp.concatenate(groups, axis=0)
        right = right_of(strip)
        own = (lane >= off) & (lane < off + STRIP)
        rest = jnp.where(own, 0.0, tile) - mm(left, right)
        parts = [rest[:off], strip, rest[off + STRIP :]]
        tile = jnp.concatenate([p for p in parts if p.shape[0]], axis=0)
    return tile


def invert_all(whole, one, pause):
    n = whole.shape[0] // TILE
    cut = lambda k: slice(k * TILE, (k + 1) * TILE)
    tiles = [[whole[cut(i), cut(j)] for j in range(n)] for i in range(n)]
    for k in range(n):
        others = [i for i in range(n) if i != k]
        inverse = invert(tiles[k][k], one, pause)
        pause()
        after = {j: mm(left_of(inverse), right_of(tiles[k][j])) for j in others}
        for i in others:
            left = left_of(tiles[i][k])
            for j in others:
                tiles[i][j] = tiles[i][j] - mm(left, right_of(after[j]))
            tiles[i][k] = -mm(left, right_of(inverse))
        for j in others:
            tiles[k][j] = after[j]
        tiles[k][k] = inverse
    return jnp.concatenate([jnp.concatenate(row, axis=1) for row in tiles], axis=0)


def gains_kernel(
    nz, nx, pred, targ, var, gains,
    dbuf, rbuf, sbuf, gbuf, pbuf, tbuf, wbuf, total, ones,
    local_sem, out_sem, zsend, xsend, csend, recv, crecv,
):
    members, width = pred.shape
    n = nz * nx * 2
    me = lax.axis_index("blk")
    core = me % 2
    x = (me // 2) % nx
    z = me // (2 * nx)
    place = lambda zo, xo, co: (zo * nx + xo) * 2 + co
    sibling = me + 1 - 2 * core

    local = (
        pltpu.make_async_copy(pred, pbuf, local_sem.at[0]),
        pltpu.make_async_copy(var, wbuf, local_sem.at[1]),
        pltpu.make_async_copy(targ, tbuf, local_sem.at[2]),
    )
    for copy in local:
        copy.start()
    ones[...] = jnp.ones_like(ones)
    total[...] = jnp.zeros_like(total)
    barrier = pltpu.get_barrier_semaphore()

    def greet(device):
        pl.semaphore_signal(barrier, inc=1, device_id={"blk": device}, device_id_type=MESH)

    for zo in range(nz):
        @pl.when(zo != z)
        def _(zo=zo):
            greet(place(zo, x, core))
    for xo in range(nx):
        @pl.when(xo != x)
        def _(xo=xo):
            greet(place(z, xo, core))
    greet(sibling)

    for copy in local:
        copy.wait()
    p = pbuf[...].astype(F32)
    db = (p - jnp.mean(p, axis=0, keepdims=True)).astype(BF16)
    dbuf[z, x, core, :members] = db
    parts = split(jnp.broadcast_to(wbuf[...], (EXTRA, width)))
    sub = lax.broadcasted_iota(jnp.int32, (EXTRA, width), 0)
    tail = jnp.where(sub == 0, parts[0].astype(F32), jnp.where(sub == 1, parts[1].astype(F32), parts[2].astype(F32)))
    dbuf[z, x, core, members:] = tail.astype(BF16)
    rbuf[z, x, core] = (tbuf[...].astype(F32) - p).astype(BF16)
    pl.semaphore_wait(barrier, nz + nx - 1)

    bufs = (dbuf, rbuf)

    def z_copy(h, to):
        block = bufs[h].at[z, x, core]
        return pltpu.make_async_remote_copy(
            src_ref=block, dst_ref=block, send_sem=zsend.at[h, to], recv_sem=recv.at[h, z, x],
            device_id={"blk": place(to, x, core)}, device_id_type=MESH,
        )

    def x_copy(h, zo, to):
        block = bufs[h].at[zo, x, core]
        return pltpu.make_async_remote_copy(
            src_ref=block, dst_ref=block, send_sem=xsend.at[h, zo, to], recv_sem=recv.at[h, zo, x],
            device_id={"blk": place(z, to, core)}, device_id_type=MESH,
        )

    def c_copy(h, xo, co):
        column = bufs[h].at[:, xo, co]
        return pltpu.make_async_remote_copy(
            src_ref=column, dst_ref=column, send_sem=csend.at[h, xo], recv_sem=crecv.at[h, xo],
            device_id={"blk": sibling}, device_id_type=MESH,
        )

    def arrive(h, zo, xo):
        block = bufs[h].at[zo, xo, core]
        pltpu.make_async_remote_copy(
            src_ref=block, dst_ref=block, send_sem=xsend.at[h, zo, xo], recv_sem=recv.at[h, zo, xo],
            device_id={"blk": sibling}, device_id_type=MESH,
        ).wait_recv()

    def each_x(fn):
        for xo in range(nx):
            @pl.when(xo != x)
            def _(xo=xo):
                fn(xo)

    def each_z(fn):
        for d in range(1, nz):
            for zo in (z - d, z + d):
                @pl.when((zo >= 0) & (zo < nz))
                def _(zo=zo):
                    fn(zo)

    def launch(h):
        each_x(lambda xo: x_copy(h, z, xo).start())
        each_z(lambda zo: z_copy(h, zo).start())

    launch(0)

    def lagged(t, lag):
        d = t // 2 - lag
        s = 1 - 2 * (t % 2)
        zo = z - s * d
        valid = (d >= 0) & (zo >= 0) & (zo < nz) & ((d > 0) | (s == 1))
        return d, zo, valid

    def forward_z(h, t):
        d, zo, valid = lagged(t, 0)

        @pl.when(valid & (d > 0))
        def _():
            arrive(h, zo, x)
            each_x(lambda xo: x_copy(h, zo, xo).start())

    def receive_x(h, t):
        _, zo, valid = lagged(t, 0)

        @pl.when(valid)
        def _():
            each_x(lambda xo: arrive(h, zo, xo))

    def at(ref, o):
        return ref.at[o // (2 * nx), (o // 2) % nx, o % 2]

    def variance(o):
        tail = at(dbuf, o)[members:].astype(F32)
        return tail[0:1] + tail[1:2] + tail[2:3]

    def absorb(zo, xo, co):
        o = place(zo, xo, co)
        block = dbuf[zo, xo, co].astype(F32)
        spread = block[members : members + 1] + block[members + 1 : members + 2] + block[members + 2 : members + 3]
        sb = (block[:members] * (1.0 / spread)).astype(BF16)
        sbuf[o] = sb
        total[...] += lax.dot_general(sb, block[:members].astype(BF16), NT, preferred_element_type=F32)

    def over_own(t, carry):
        forward_z(0, t)

        @pl.when(t == 2 * nz - 1)
        def _():
            c_copy(0, x, core).start()
            launch(1)
        _, zo, valid = lagged(t, 0)

        @pl.when(valid)
        def _():
            absorb(zo, x, core)
        return carry

    def over_far(t, carry):
        receive_x(0, t)
        return carry

    def send_far(h):
        each_x(lambda xo: c_copy(h, xo, core).start())

    lax.fori_loop(0, 2 * nz, over_own, 0)

    def absorb_column(xo, co):
        def one(zo, carry):
            absorb(zo, xo, co)
            return carry
        lax.fori_loop(0, nz, one, 0)

    def absorb_sent(xo):
        c_copy(0, xo, 1 - core).wait_recv()
        absorb_column(xo, 1 - core)

    absorb_sent(x)
    lax.fori_loop(0, 2 * nz, over_far, 0)
    send_far(0)
    each_x(lambda xo: absorb_column(xo, core))
    each_x(absorb_sent)

    count = [0]

    def relay(fn, spots):
        first, last = spots

        def one(t, carry):
            fn(t)
            return carry

        for d in range(nz):
            spot = first + (last - first) * d // (nz - 1)
            if spot == count[0]:
                lax.fori_loop(2 * d, 2 * d + 2, one, 0)

    def pause():
        relay(lambda t: forward_z(1, t), Z_SPOTS)
        if count[0] == Z_SPOTS[1]:
            c_copy(1, x, core).start()
        relay(lambda t: receive_x(1, t), X_SPOTS)
        if count[0] == X_SPOTS[1]:
            send_far(1)
        count[0] += 1

    row = lax.broadcasted_iota(jnp.int32, total.shape, 0)
    col = lax.broadcasted_iota(jnp.int32, total.shape, 1)
    whole = total[...] + jnp.where(row == col, members - 1.0, 0.0)
    pause()
    inverse = right_of(invert_all(whole, ones[...], pause))

    for xo in range(nx):
        c_copy(1, xo, 1 - core).wait_recv()

    group = min(n, 16)

    def gather_cross(g, carry):
        left = jnp.concatenate([at(rbuf, g * group + i)[...] for i in range(group)], axis=1)
        right = jnp.concatenate([sbuf[g * group + i] for i in range(group)], axis=1)
        product = lax.dot_general(left, right, NT, preferred_element_type=F32)
        total[...] = jnp.where(g == 0, product, total[...] + product)
        return carry

    lax.fori_loop(0, n // group, gather_cross, 0)
    xt = mm(left_of(total[...]), inverse)
    stack = jnp.concatenate(split(xt), axis=0)

    def innovate(g, carry):
        for i in range(0, group, 2):
            o = g * group + i
            d = jnp.concatenate([at(dbuf, o)[:members], at(dbuf, o + 1)[:members]], axis=1)
            r = jnp.concatenate([at(rbuf, o)[...], at(rbuf, o + 1)[...]], axis=1).astype(F32)
            w = jnp.concatenate([variance(o), variance(o + 1)], axis=1)
            w = 1.0 / (w * (members - 1.0))
            parts = mm(stack, d)
            update = parts[:members] + (parts[members : 2 * members] + parts[2 * members :])
            v = ((r - update) * w).astype(BF16)
            sbuf[o] = v[:, :width]
            sbuf[o + 1] = v[:, width:]
        return carry

    def out_copy(o):
        return pltpu.make_async_copy(gbuf.at[o], gains.at[o], out_sem.at[o])

    def gain(g, carry):
        for i in range(group):
            o = g * group + i
            product = lax.dot_general(sbuf[o], at(dbuf, o)[:members], NT, preferred_element_type=F32)
            gbuf[o] = product.astype(BF16)
            out_copy(o).start()
        return carry

    lax.fori_loop(0, n // group, innovate, 0)
    lax.fori_loop(0, n // group, gain, 0)

    def drain(h):
        each_z(lambda zo: z_copy(h, zo).wait_send())

        def over_z(zo, carry):
            each_x(lambda xo: x_copy(h, zo, xo).wait_send())
            return carry
        lax.fori_loop(0, nz, over_z, 0)

        for xo in range(nx):
            c_copy(h, xo, core).wait_send()

    drain(0)
    drain(1)

    def stored(o, carry):
        out_copy(o).wait()
        return carry

    lax.fori_loop(0, n, stored, 0)


def all_gains(n, pred, targ, var):
    nz, nx = chip_grid(n)
    members, width = pred.shape
    hbm = pl.BlockSpec(memory_space=pltpu.HBM)
    sem = pltpu.SemaphoreType.DMA
    return pl.pallas_call(
        functools.partial(gains_kernel, nz, nx),
        out_shape=jax.ShapeDtypeStruct((n + SPARE, members, members), BF16),
        in_specs=[hbm, hbm, hbm],
        out_specs=hbm,
        scratch_shapes=[
            pltpu.VMEM((nz, nx, 2, members + EXTRA, width), BF16),
            pltpu.VMEM((nz, nx, 2, members, width), BF16),
            pltpu.VMEM((n, members, width), BF16),
            pltpu.VMEM((n, members, members), BF16),
            pltpu.VMEM((members, width), BF16),
            pltpu.VMEM((members, width), BF16),
            pltpu.VMEM((1, width), F32),
            pltpu.VMEM((members, members), F32),
            pltpu.VMEM((8, TILE), F32),
            sem((3,)), sem((n,)), sem((2, nz)), sem((2, nz, nx)), sem((2, nx)), sem((2, nz, nx)), sem((2, nx)),
        ],
        compiler_params=pltpu.CompilerParams(
            collective_id=0, has_side_effects=True, vmem_limit_bytes=VMEM
        ),
        name="gather_gains",
    )(pred, targ, var)


def step_kernel(
    ids, far_gains, pair, taper, ens, out,
    gains, mixer, gain_sum, uanom, result, gain_sem, sems,
):
    slots, members, _ = gains.shape
    blocks = pair.shape[0]
    cell = ens.shape[1] // blocks
    piece = members // PIECES
    gain_copies = []
    for k in range(PIECES):
        some = pl.ds(k * piece, piece)
        gain_copies.append(
            pltpu.make_async_copy(far_gains.at[pl.ds(0, slots), some], gains.at[:, some], gain_sem.at[k])
        )
        gain_copies[-1].start()
    pairs = pair[...]
    tapers = taper[...]
    spread = ROWS * slots
    lane = lax.broadcasted_iota(jnp.int32, (blocks, spread), 1)
    weight = jnp.zeros((blocks, spread), F32)
    for s in range(slots):
        hit = jnp.where(pairs == ids[s], tapers, 0.0)
        both = jnp.sum(hit, axis=1, keepdims=True)
        weight = jnp.where(lane // ROWS == s, both, weight)
    sub = lax.broadcasted_iota(jnp.int32, (ROWS, spread), 0)
    spot = lax.broadcasted_iota(jnp.int32, (ROWS, spread), 1) % ROWS == sub
    for c in range(blocks):
        row = jnp.broadcast_to(weight[c : c + 1, :], (ROWS, spread))
        mixer[c * ROWS : (c + 1) * ROWS, :] = jnp.where(spot, row, 0.0).astype(BF16)
    mix = mixer[...]
    strips = members // ROWS
    for c in range(blocks):
        u = ens[:, c * cell : (c + 1) * cell].astype(F32)
        uanom[:, c * cell : (c + 1) * cell] = (u - jnp.mean(u, axis=0, keepdims=True)).astype(BF16)
    for i in range(strips):
        if i * ROWS % piece == 0:
            gain_copies[i * ROWS // piece].wait()
        rows = slice(i * ROWS, (i + 1) * ROWS)
        stack = gains[:, rows, :].reshape(slots * ROWS, members)
        mixed = jnp.dot(mix, stack, preferred_element_type=F32).astype(BF16)
        gain_sum[:, rows, :] = mixed.reshape(blocks, ROWS, members)
    copies = []
    for first in range(0, blocks, TOGETHER):
        for c in range(first, first + TOGETHER):
            cols = slice(c * cell, (c + 1) * cell)
            result[:, cols] = jnp.dot(gain_sum[c], uanom[:, cols], preferred_element_type=F32)
        cols = pl.ds(first * cell, TOGETHER * cell)
        copies.append(pltpu.make_async_copy(result.at[:, cols], out.at[:, cols], sems.at[len(copies)]))
        copies[-1].start()
    for copy in copies:
        copy.wait()


def finish(ensemble, gains, ids, pair, taper):
    members, cells = ensemble.shape
    blocks = pair.shape[0]
    slots = ids.shape[0]
    hbm = pl.BlockSpec(memory_space=pltpu.HBM)
    vmem = pl.BlockSpec(memory_space=pltpu.VMEM)
    return pl.pallas_call(
        step_kernel,
        out_shape=jax.ShapeDtypeStruct((members, cells), F32),
        in_specs=[pl.BlockSpec(memory_space=pltpu.SMEM), hbm, vmem, vmem, vmem],
        out_specs=hbm,
        scratch_shapes=[
            pltpu.VMEM((slots, members, members), BF16),
            pltpu.VMEM((blocks * ROWS, slots * ROWS), BF16),
            pltpu.VMEM((blocks, members, members), BF16),
            pltpu.VMEM((members, cells), BF16),
            pltpu.VMEM((members, cells), F32),
            pltpu.SemaphoreType.DMA((PIECES,)),
            pltpu.SemaphoreType.DMA((blocks // TOGETHER,)),
        ],
        compiler_params=pltpu.CompilerParams(vmem_limit_bytes=48 << 20),
        name="mix_step",
    )(ids, gains, pair, taper, ensemble)


def solution(mesh):
    n = mesh.shape["blk"]

    def per_device(ensemble, predicted, targets, datum_noise_variance, block_ids, pair_blocks, taper):
        gains = all_gains(n, predicted, targets, datum_noise_variance.reshape(1, -1))
        return finish(ensemble, gains, block_ids, pair_blocks, taper)

    in_specs = (
        P(None, ("groups", "blk")),
        P(None, ("groups", "blk")),
        P(None, ("groups", "blk")),
        P(("groups", "blk")),
        P("groups"),
        P(("groups", "blk"), None),
        P(("groups", "blk"), None),
    )
    return jax.shard_map(
        per_device, mesh=mesh, in_specs=in_specs, out_specs=P(None, ("groups", "blk")), check_vma=False
    )
```

```python
import functools

import jax
import jax.numpy as jnp
from jax import lax
from jax.experimental import pallas as pl
from jax.experimental.pallas import tpu as pltpu
from jax.sharding import PartitionSpec as P

MESH = pl.DeviceIdType.MESH
F32 = jnp.float32
BF16 = jnp.bfloat16
NT = (((1,), (1,)), ((), ()))
TILE = 128
EXTRA = 16
BATCH = 2
SPARE = 64
PIECES = 2
PACE = 32
Z_SPOTS = (0, 0, 1, 2)
X_SPOTS = (4, 4, 6, 6)
VMEM = 54 << 20
TOGETHER = 2
STRIP = 16
ROWS = 16


def chip_grid(n):
    chips = n // 2
    nx = max(f for f in range(1, chips + 1) if chips % f == 0 and f * f * f <= chips)
    return chips // nx, nx


def rows_of(value, j):
    return jnp.broadcast_to(value[j : j + 1, :], value.shape)


def lanes_of(value, j):
    return jnp.broadcast_to(value[:, j : j + 1], value.shape)


def tree(parts):
    while len(parts) > 1:
        parts = [parts[i] + parts[i + 1] for i in range(0, len(parts), 2)]
    return parts[0]
def split(value):
    high = value.astype(BF16)
    rest = value - high.astype(F32)
    mid = rest.astype(BF16)
    return high, mid, (rest - mid.astype(F32)).astype(BF16)
def left_of(value):
    high, mid, low = split(value)
    return jnp.concatenate([high, high, mid, mid, high, low], axis=1)
def right_of(value):
    high, mid, low = split(value)
    return jnp.concatenate([high, mid, high, mid, low, high], axis=0)
def mm(left, right):
    return jnp.dot(left, right, preferred_element_type=F32)

def pivot_pair(j, cols, rows, sub):
    k = j + 1
    first, second = sub == j, sub == k
    pair = first | second
    a, b, c = rows_of(cols[j], j), rows_of(cols[k], j), rows_of(cols[k], k)
    ia = 1.0 / a
    isc = a * (1.0 / (a * c - b * b))
    cj = jnp.where(first, -1.0, jnp.where(second, 0.0, cols[j]))
    ck = jnp.where(second, -1.0, jnp.where(first, 0.0, cols[k])) - (cj * b) * ia
    bia, cja, cks = b * ia, cj * ia, ck * isc
    def reduce(t, soon):
        tj, tk = rows_of(t, j), rows_of(t, k)
        base = jnp.where(pair, 0.0, t)
        if soon:
            return base - (cj * tj) * ia - (ck * (tk - (b * tj) * ia)) * isc
        return base - cja * tj - cks * (tk - bia * tj)
    return [reduce(t, m <= k + 2) if m > k else t for m, t in enumerate(cols)], reduce(rows, False)

def sweep(groups, off, one):
    lane = lax.broadcasted_iota(jnp.int32, (8, TILE), 1)
    sub = lax.broadcasted_iota(jnp.int32, (8, TILE), 0)
    groups = list(groups)
    n = len(groups)
    for q in range(n):
        at = off + 8 * q
        here = (lane >= at) & (lane < at + 8)
        cols = [lanes_of(groups[q], at + j) * one for j in range(8)]
        rows = jnp.where(here, jnp.where(lane - at == sub, 1.0, 0.0), groups[q])
        for j in range(0, 8, 2):
            cols, rows = pivot_pair(j, cols, rows, sub)
        final = [rows_of(rows, j) for j in range(8)]
        for r in [(q + 1 + i) % n for i in range(n - 1)]:
            take = tree([lanes_of(groups[r], at + j) * final[j] for j in range(8)])
            groups[r] = jnp.where(here, 0.0, groups[r]) - take
        groups[q] = rows
    return groups

def invert(tile, one, pause):
    size = tile.shape[0]
    lane = lax.broadcasted_iota(jnp.int32, tile.shape, 1)
    for off in range(0, size, STRIP):
        if off and off % PACE == 0:
            pause()
        left = left_of(tile[:, off : off + STRIP])
        groups = sweep([tile[off + 8 * r : off + 8 * r + 8, :] for r in range(STRIP // 8)], off, one)
        strip = jnp.concatenate(groups, axis=0)
        right = right_of(strip)
        own = (lane >= off) & (lane < off + STRIP)
        rest = jnp.where(own, 0.0, tile) - mm(left, right)
        parts = [rest[:off], strip, rest[off + STRIP :]]
        tile = jnp.concatenate([p for p in parts if p.shape[0]], axis=0)
    return tile


def invert_all(whole, one, pause):
    n = whole.shape[0] // TILE
    cut = lambda k: slice(k * TILE, (k + 1) * TILE)
    tiles = [[whole[cut(i), cut(j)] for j in range(n)] for i in range(n)]
    for k in range(n):
        others = [i for i in range(n) if i != k]
        inverse = invert(tiles[k][k], one, pause)
        pause()
        after = {j: mm(left_of(inverse), right_of(tiles[k][j])) for j in others}
        for i in others:
            left = left_of(tiles[i][k])
            for j in others:
                tiles[i][j] = tiles[i][j] - mm(left, right_of(after[j]))
            tiles[i][k] = -mm(left, right_of(inverse))
        for j in others:
            tiles[k][j] = after[j]
        tiles[k][k] = inverse
    return jnp.concatenate([jnp.concatenate(row, axis=1) for row in tiles], axis=0)


def gains_kernel(
    nz, nx, pred, targ, var, gains,
    dbuf, rbuf, sbuf, gbuf, pbuf, tbuf, wbuf, total, ones,
    local_sem, out_sem, zsend, xsend, csend, recv, crecv,
):
    members, width = pred.shape
    n = nz * nx * 2
    me = lax.axis_index("blk")
    core = me % 2
    x = (me // 2) % nx
    z = me // (2 * nx)
    place = lambda zo, xo, co: (zo * nx + xo) * 2 + co
    sibling = me + 1 - 2 * core

    local = (
        pltpu.make_async_copy(pred, pbuf, local_sem.at[0]),
        pltpu.make_async_copy(var, wbuf, local_sem.at[1]),
        pltpu.make_async_copy(targ, tbuf, local_sem.at[2]),
    )
    for copy in local:
        copy.start()
    ones[...] = jnp.ones_like(ones)
    total[...] = jnp.zeros_like(total)
    barrier = pltpu.get_barrier_semaphore()

    def greet(device):
        pl.semaphore_signal(barrier, inc=1, device_id={"blk": device}, device_id_type=MESH)

    for zo in range(nz):
        @pl.when(zo != z)
        def _(zo=zo):
            greet(place(zo, x, core))
    for xo in range(nx):
        @pl.when(xo != x)
        def _(xo=xo):
            greet(place(z, xo, core))
    greet(sibling)

    for copy in local:
        copy.wait()
    p = pbuf[...].astype(F32)
    db = (p - jnp.mean(p, axis=0, keepdims=True)).astype(BF16)
    dbuf[z, x, core, :members] = db
    parts = split(jnp.broadcast_to(wbuf[...], (EXTRA, width)))
    sub = lax.broadcasted_iota(jnp.int32, (EXTRA, width), 0)
    tail = jnp.where(sub == 0, parts[0].astype(F32), jnp.where(sub == 1, parts[1].astype(F32), parts[2].astype(F32)))
    dbuf[z, x, core, members:] = tail.astype(BF16)
    rbuf[z, x, core] = (tbuf[...].astype(F32) - p).astype(BF16)
    pl.semaphore_wait(barrier, nz + nx - 1)

    bufs = (dbuf, rbuf)

    def z_copy(h, to):
        block = bufs[h].at[z, x, core]
        return pltpu.make_async_remote_copy(
            src_ref=block, dst_ref=block, send_sem=zsend.at[h, to], recv_sem=recv.at[h, z, x],
            device_id={"blk": place(to, x, core)}, device_id_type=MESH,
        )

    def x_copy(h, zo, to):
        block = bufs[h].at[zo, x, core]
        return pltpu.make_async_remote_copy(
            src_ref=block, dst_ref=block, send_sem=xsend.at[h, zo, to], recv_sem=recv.at[h, zo, x],
            device_id={"blk": place(z, to, core)}, device_id_type=MESH,
        )

    def c_copy(h, xo, co):
        column = bufs[h].at[:, xo, co]
        return pltpu.make_async_remote_copy(
            src_ref=column, dst_ref=column, send_sem=csend.at[h, xo], recv_sem=crecv.at[h, xo],
            device_id={"blk": sibling}, device_id_type=MESH,
        )

    def arrive(h, zo, xo):
        block = bufs[h].at[zo, xo, core]
        pltpu.make_async_remote_copy(
            src_ref=block, dst_ref=block, send_sem=xsend.at[h, zo, xo], recv_sem=recv.at[h, zo, xo],
            device_id={"blk": sibling}, device_id_type=MESH,
        ).wait_recv()

    def each_x(fn):
        for xo in range(nx):
            @pl.when(xo != x)
            def _(xo=xo):
                fn(xo)

    def each_z(fn):
        for d in range(1, nz):
            for zo in (z - d, z + d):
                @pl.when((zo >= 0) & (zo < nz))
                def _(zo=zo):
                    fn(zo)

    def launch(h):
        each_x(lambda xo: x_copy(h, z, xo).start())
        each_z(lambda zo: z_copy(h, zo).start())

    launch(0)

    def lagged(t, lag):
        d = t // 2 - lag
        s = 1 - 2 * (t % 2)
        zo = z - s * d
        valid = (d >= 0) & (zo >= 0) & (zo < nz) & ((d > 0) | (s == 1))
        return d, zo, valid

    def forward_z(h, t):
        d, zo, valid = lagged(t, 0)

        @pl.when(valid & (d > 0))
        def _():
            arrive(h, zo, x)
            each_x(lambda xo: x_copy(h, zo, xo).start())

    def receive_x(h, t):
        _, zo, valid = lagged(t, 0)

        @pl.when(valid)
        def _():
            each_x(lambda xo: arrive(h, zo, xo))

    def at(ref, o):
        return ref.at[o // (2 * nx), (o // 2) % nx, o % 2]

    def variance(o):
        tail = at(dbuf, o)[members:].astype(F32)
        return tail[0:1] + tail[1:2] + tail[2:3]

    def absorb_all(places):
        scaled, plain = [], []
        for zo, xo, co in places:
            o = place(zo, xo, co)
            db = dbuf[zo, xo, co, :members]
            tail = dbuf[zo, xo, co, members:].astype(F32)
            sb = (db.astype(F32) * (1.0 / (tail[0:1] + tail[1:2] + tail[2:3]))).astype(BF16)
            sbuf[o] = sb
            scaled.append(sb)
            plain.append(db)
        left, right = jnp.concatenate(scaled, axis=1), jnp.concatenate(plain, axis=1)
        total[...] += lax.dot_general(left, right, NT, preferred_element_type=F32)

    def absorb(zo, xo, co):
        absorb_all([(zo, xo, co)])

    def over_own(t, carry):
        forward_z(0, t)

        @pl.when(t == 2 * nz - 1)
        def _():
            c_copy(0, x, core).start()
            launch(1)
        _, zo, valid = lagged(t, 0)

        @pl.when(valid)
        def _():
            absorb(zo, x, core)
        return carry

    def over_far(t, carry):
        receive_x(0, t)
        return carry

    def send_far(h):
        each_x(lambda xo: c_copy(h, xo, core).start())

    lax.fori_loop(0, 2 * nz, over_own, 0)

    def absorb_column(xo, co):
        for first in range(0, nz, BATCH):
            absorb_all([(zo, xo, co) for zo in range(first, min(first + BATCH, nz))])

    def absorb_sent(xo):
        c_copy(0, xo, 1 - core).wait_recv()
        absorb_column(xo, 1 - core)

    absorb_sent(x)
    lax.fori_loop(0, 2 * nz, over_far, 0)
    send_far(0)
    each_x(lambda xo: absorb_column(xo, core))
    each_x(absorb_sent)

    count = [0]

    def relay(fn, spots):

        def one(t, carry):
            fn(t)
            return carry

        for d in range(nz):
            if spots[d * len(spots) // nz] == count[0]:
                lax.fori_loop(2 * d, 2 * d + 2, one, 0)

    def pause():
        relay(lambda t: forward_z(1, t), Z_SPOTS)
        if count[0] == Z_SPOTS[-1]:
            c_copy(1, x, core).start()
        relay(lambda t: receive_x(1, t), X_SPOTS)
        if count[0] == X_SPOTS[-1]:
            send_far(1)
        count[0] += 1

    row = lax.broadcasted_iota(jnp.int32, total.shape, 0)
    col = lax.broadcasted_iota(jnp.int32, total.shape, 1)
    whole = total[...] + jnp.where(row == col, members - 1.0, 0.0)
    pause()
    inverse = right_of(invert_all(whole, ones[...], pause))

    for xo in range(nx):
        c_copy(1, xo, 1 - core).wait_recv()

    group = min(n, 16)

    def gather_cross(g, carry):
        left = jnp.concatenate([at(rbuf, g * group + i)[...] for i in range(group)], axis=1)
        right = jnp.concatenate([sbuf[g * group + i] for i in range(group)], axis=1)
        product = lax.dot_general(left, right, NT, preferred_element_type=F32)
        total[...] = jnp.where(g == 0, product, total[...] + product)
        return carry

    lax.fori_loop(0, n // group, gather_cross, 0)
    xt = mm(left_of(total[...]), inverse)
    stack = jnp.concatenate(split(xt), axis=0)

    def innovate(g, carry):
        for i in range(0, group, 2):
            o = g * group + i
            d = jnp.concatenate([at(dbuf, o)[:members], at(dbuf, o + 1)[:members]], axis=1)
            r = jnp.concatenate([at(rbuf, o)[...], at(rbuf, o + 1)[...]], axis=1).astype(F32)
            w = jnp.concatenate([variance(o), variance(o + 1)], axis=1)
            w = 1.0 / (w * (members - 1.0))
            parts = mm(stack, d)
            update = parts[:members] + (parts[members : 2 * members] + parts[2 * members :])
            v = ((r - update) * w).astype(BF16)
            sbuf[o] = v[:, :width]
            sbuf[o + 1] = v[:, width:]
        return carry

    def out_copy(o):
        return pltpu.make_async_copy(gbuf.at[o], gains.at[o], out_sem.at[o])

    def gain(g, carry):
        for i in range(group):
            o = g * group + i
            product = lax.dot_general(sbuf[o], at(dbuf, o)[:members], NT, preferred_element_type=F32)
            gbuf[o] = product.astype(BF16)
            out_copy(o).start()
        return carry

    lax.fori_loop(0, n // group, innovate, 0)
    lax.fori_loop(0, n // group, gain, 0)

    def drain(h):
        each_z(lambda zo: z_copy(h, zo).wait_send())

        def over_z(zo, carry):
            each_x(lambda xo: x_copy(h, zo, xo).wait_send())
            return carry
        lax.fori_loop(0, nz, over_z, 0)

        for xo in range(nx):
            c_copy(h, xo, core).wait_send()

    drain(0)
    drain(1)

    def stored(o, carry):
        out_copy(o).wait()
        return carry

    lax.fori_loop(0, n, stored, 0)


def all_gains(n, pred, targ, var):
    nz, nx = chip_grid(n)
    members, width = pred.shape
    hbm = pl.BlockSpec(memory_space=pltpu.HBM)
    sem = pltpu.SemaphoreType.DMA
    return pl.pallas_call(
        functools.partial(gains_kernel, nz, nx),
        out_shape=jax.ShapeDtypeStruct((n + SPARE, members, members), BF16),
        in_specs=[hbm, hbm, hbm],
        out_specs=hbm,
        scratch_shapes=[
            pltpu.VMEM((nz, nx, 2, members + EXTRA, width), BF16),
            pltpu.VMEM((nz, nx, 2, members, width), BF16),
            pltpu.VMEM((n, members, width), BF16),
            pltpu.VMEM((n, members, members), BF16),
            pltpu.VMEM((members, width), BF16),
            pltpu.VMEM((members, width), BF16),
            pltpu.VMEM((1, width), F32),
            pltpu.VMEM((members, members), F32),
            pltpu.VMEM((8, TILE), F32),
            sem((3,)), sem((n,)), sem((2, nz)), sem((2, nz, nx)), sem((2, nx)), sem((2, nz, nx)), sem((2, nx)),
        ],
        compiler_params=pltpu.CompilerParams(
            collective_id=0, has_side_effects=True, vmem_limit_bytes=VMEM
        ),
        name="gather_gains",
    )(pred, targ, var)


def step_kernel(
    ids, far_gains, pair, taper, ens, out,
    gains, mixer, gain_sum, uanom, result, gain_sem, sems,
):
    slots, members, _ = gains.shape
    blocks = pair.shape[0]
    cell = ens.shape[1] // blocks
    piece = members // PIECES
    gain_copies = []
    for k in range(PIECES):
        some = pl.ds(k * piece, piece)
        gain_copies.append(
            pltpu.make_async_copy(far_gains.at[pl.ds(0, slots), some], gains.at[:, some], gain_sem.at[k])
        )
        gain_copies[-1].start()
    pairs = pair[...]
    tapers = taper[...]
    spread = ROWS * slots
    lane = lax.broadcasted_iota(jnp.int32, (blocks, spread), 1)
    weight = jnp.zeros((blocks, spread), F32)
    for s in range(slots):
        hit = jnp.where(pairs == ids[s], tapers, 0.0)
        both = jnp.sum(hit, axis=1, keepdims=True)
        weight = jnp.where(lane // ROWS == s, both, weight)
    sub = lax.broadcasted_iota(jnp.int32, (ROWS, spread), 0)
    spot = lax.broadcasted_iota(jnp.int32, (ROWS, spread), 1) % ROWS == sub
    for c in range(blocks):
        row = jnp.broadcast_to(weight[c : c + 1, :], (ROWS, spread))
        mixer[c * ROWS : (c + 1) * ROWS, :] = jnp.where(spot, row, 0.0).astype(BF16)
    mix = mixer[...]
    strips = members // ROWS
    for c in range(blocks):
        u = ens[:, c * cell : (c + 1) * cell].astype(F32)
        uanom[:, c * cell : (c + 1) * cell] = (u - jnp.mean(u, axis=0, keepdims=True)).astype(BF16)
    for i in range(strips):
        if i * ROWS % piece == 0:
            gain_copies[i * ROWS // piece].wait()
        rows = slice(i * ROWS, (i + 1) * ROWS)
        stack = gains[:, rows, :].reshape(slots * ROWS, members)
        mixed = jnp.dot(mix, stack, preferred_element_type=F32).astype(BF16)
        gain_sum[:, rows, :] = mixed.reshape(blocks, ROWS, members)
    copies = []
    for first in range(0, blocks, TOGETHER):
        for c in range(first, first + TOGETHER):
            cols = slice(c * cell, (c + 1) * cell)
            result[:, cols] = jnp.dot(gain_sum[c], uanom[:, cols], preferred_element_type=F32)
        cols = pl.ds(first * cell, TOGETHER * cell)
        copies.append(pltpu.make_async_copy(result.at[:, cols], out.at[:, cols], sems.at[len(copies)]))
        copies[-1].start()
    for copy in copies:
        copy.wait()


def finish(ensemble, gains, ids, pair, taper):
    members, cells = ensemble.shape
    blocks = pair.shape[0]
    slots = ids.shape[0]
    hbm = pl.BlockSpec(memory_space=pltpu.HBM)
    vmem = pl.BlockSpec(memory_space=pltpu.VMEM)
    return pl.pallas_call(
        step_kernel,
        out_shape=jax.ShapeDtypeStruct((members, cells), F32),
        in_specs=[pl.BlockSpec(memory_space=pltpu.SMEM), hbm, vmem, vmem, vmem],
        out_specs=hbm,
        scratch_shapes=[
            pltpu.VMEM((slots, members, members), BF16),
            pltpu.VMEM((blocks * ROWS, slots * ROWS), BF16),
            pltpu.VMEM((blocks, members, members), BF16),
            pltpu.VMEM((members, cells), BF16),
            pltpu.VMEM((members, cells), F32),
            pltpu.SemaphoreType.DMA((PIECES,)),
            pltpu.SemaphoreType.DMA((blocks // TOGETHER,)),
        ],
        compiler_params=pltpu.CompilerParams(vmem_limit_bytes=48 << 20),
        name="mix_step",
    )(ids, gains, pair, taper, ensemble)


def solution(mesh):
    n = mesh.shape["blk"]

    def per_device(ensemble, predicted, targets, datum_noise_variance, block_ids, pair_blocks, taper):
        gains = all_gains(n, predicted, targets, datum_noise_variance.reshape(1, -1))
        return finish(ensemble, gains, block_ids, pair_blocks, taper)

    in_specs = (
        P(None, ("groups", "blk")),
        P(None, ("groups", "blk")),
        P(None, ("groups", "blk")),
        P(("groups", "blk")),
        P("groups"),
        P(("groups", "blk"), None),
        P(("groups", "blk"), None),
    )
    return jax.shard_map(
        per_device, mesh=mesh, in_specs=in_specs, out_specs=P(None, ("groups", "blk")), check_vma=False
    )
```

```python
import functools

import jax
import jax.numpy as jnp
from jax import lax
from jax.experimental import pallas as pl
from jax.experimental.pallas import tpu as pltpu
from jax.sharding import PartitionSpec as P

MESH = pl.DeviceIdType.MESH
F32 = jnp.float32
BF16 = jnp.bfloat16
NT = (((1,), (1,)), ((), ()))
TILE = 128
EXTRA = 16
BATCH = 2
SPARE = 64
PIECES = 2
PACE = 32
Z_SPOTS = (0, 0, 1, 2)
X_SPOTS = (4, 4, 6, 6)
VMEM = 54 << 20
TOGETHER = 2
STRIP = 16
ROWS = 16


def chip_grid(n):
    chips = n // 2
    nx = max(f for f in range(1, chips + 1) if chips % f == 0 and f * f * f <= chips)
    return chips // nx, nx


def rows_of(value, j):
    return jnp.broadcast_to(value[j : j + 1, :], value.shape)


def lanes_of(value, j):
    return jnp.broadcast_to(value[:, j : j + 1], value.shape)


def tree(parts):
    while len(parts) > 1:
        parts = [parts[i] + parts[i + 1] for i in range(0, len(parts), 2)]
    return parts[0]
def split(value):
    high = value.astype(BF16)
    rest = value - high.astype(F32)
    mid = rest.astype(BF16)
    return high, mid, (rest - mid.astype(F32)).astype(BF16)
def left_of(value):
    high, mid, low = split(value)
    return jnp.concatenate([high, high, mid, mid, high, low], axis=1)
def right_of(value):
    high, mid, low = split(value)
    return jnp.concatenate([high, mid, high, mid, low, high], axis=0)
def mm(left, right):
    return jnp.dot(left, right, preferred_element_type=F32)

def pivot_pair(j, cols, rows, sub):
    k = j + 1
    first, second = sub == j, sub == k
    pair = first | second
    a, b, c = rows_of(cols[j], j), rows_of(cols[k], j), rows_of(cols[k], k)
    ia = 1.0 / a
    isc = a * (1.0 / (a * c - b * b))
    cj = jnp.where(first, -1.0, jnp.where(second, 0.0, cols[j]))
    ck = jnp.where(second, -1.0, jnp.where(first, 0.0, cols[k])) - (cj * b) * ia
    bia, cja, cks = b * ia, cj * ia, ck * isc
    def reduce(t, soon):
        tj, tk = rows_of(t, j), rows_of(t, k)
        base = jnp.where(pair, 0.0, t)
        if soon:
            return base - (cj * tj) * ia - (ck * (tk - (b * tj) * ia)) * isc
        return base - cja * tj - cks * (tk - bia * tj)
    return [reduce(t, m <= k + 2) if m > k else t for m, t in enumerate(cols)], reduce(rows, False)

def sweep(groups, off, one):
    lane = lax.broadcasted_iota(jnp.int32, (8, TILE), 1)
    sub = lax.broadcasted_iota(jnp.int32, (8, TILE), 0)
    groups = list(groups)
    n = len(groups)
    for q in range(n):
        at = off + 8 * q
        here = (lane >= at) & (lane < at + 8)
        cols = [lanes_of(groups[q], at + j) * one for j in range(8)]
        rows = jnp.where(here, jnp.where(lane - at == sub, 1.0, 0.0), groups[q])
        for j in range(0, 8, 2):
            cols, rows = pivot_pair(j, cols, rows, sub)
        final = [rows_of(rows, j) for j in range(8)]
        for r in [(q + 1 + i) % n for i in range(n - 1)]:
            take = tree([lanes_of(groups[r], at + j) * final[j] for j in range(8)])
            groups[r] = jnp.where(here, 0.0, groups[r]) - take
        groups[q] = rows
    return groups

def invert(tile, one, pause):
    size = tile.shape[0]
    lane = lax.broadcasted_iota(jnp.int32, tile.shape, 1)
    for off in range(0, size, STRIP):
        if off and off % PACE == 0:
            pause()
        left = left_of(tile[:, off : off + STRIP])
        groups = sweep([tile[off + 8 * r : off + 8 * r + 8, :] for r in range(STRIP // 8)], off, one)
        strip = jnp.concatenate(groups, axis=0)
        right = right_of(strip)
        own = (lane >= off) & (lane < off + STRIP)
        rest = jnp.where(own, 0.0, tile) - mm(left, right)
        parts = [rest[:off], strip, rest[off + STRIP :]]
        tile = jnp.concatenate([p for p in parts if p.shape[0]], axis=0)
    return tile


def invert_all(whole, one, pause):
    n = whole.shape[0] // TILE
    cut = lambda k: slice(k * TILE, (k + 1) * TILE)
    tiles = [[whole[cut(i), cut(j)] for j in range(n)] for i in range(n)]
    for k in range(n):
        others = [i for i in range(n) if i != k]
        inverse = invert(tiles[k][k], one, pause)
        pause()
        after = {j: mm(left_of(inverse), right_of(tiles[k][j])) for j in others}
        for i in others:
            left = left_of(tiles[i][k])
            for j in others:
                tiles[i][j] = tiles[i][j] - mm(left, right_of(after[j]))
            tiles[i][k] = -mm(left, right_of(inverse))
        for j in others:
            tiles[k][j] = after[j]
        tiles[k][k] = inverse
    return jnp.concatenate([jnp.concatenate(row, axis=1) for row in tiles], axis=0)


def gains_kernel(
    nz, nx, pred, targ, var, gains,
    dbuf, rbuf, sbuf, gbuf, pbuf, tbuf, wbuf, total, ones,
    local_sem, out_sem, zsend, xsend, csend, recv, crecv,
):
    members, width = pred.shape
    n = nz * nx * 2
    me = lax.axis_index("blk")
    core = me % 2
    x = (me // 2) % nx
    z = me // (2 * nx)
    place = lambda zo, xo, co: (zo * nx + xo) * 2 + co
    sibling = me + 1 - 2 * core

    local = (
        pltpu.make_async_copy(pred, pbuf, local_sem.at[0]),
        pltpu.make_async_copy(var, wbuf, local_sem.at[1]),
        pltpu.make_async_copy(targ, tbuf, local_sem.at[2]),
    )
    for copy in local:
        copy.start()
    ones[...] = jnp.ones_like(ones)
    total[...] = jnp.zeros_like(total)
    barrier = pltpu.get_barrier_semaphore()

    def greet(device):
        pl.semaphore_signal(barrier, inc=1, device_id={"blk": device}, device_id_type=MESH)

    for zo in range(nz):
        @pl.when(zo != z)
        def _(zo=zo):
            greet(place(zo, x, core))
    for xo in range(nx):
        @pl.when(xo != x)
        def _(xo=xo):
            greet(place(z, xo, core))
    greet(sibling)

    for copy in local:
        copy.wait()
    p = pbuf[...].astype(F32)
    db = (p - jnp.mean(p, axis=0, keepdims=True)).astype(BF16)
    dbuf[z, x, core, :members] = db
    parts = split(jnp.broadcast_to(wbuf[...], (EXTRA, width)))
    sub = lax.broadcasted_iota(jnp.int32, (EXTRA, width), 0)
    tail = jnp.where(sub == 0, parts[0].astype(F32), jnp.where(sub == 1, parts[1].astype(F32), parts[2].astype(F32)))
    dbuf[z, x, core, members:] = tail.astype(BF16)
    rbuf[z, x, core] = (tbuf[...].astype(F32) - p).astype(BF16)
    pl.semaphore_wait(barrier, nz + nx - 1)

    bufs = (dbuf, rbuf)

    def z_copy(h, to):
        block = bufs[h].at[z, x, core]
        return pltpu.make_async_remote_copy(
            src_ref=block, dst_ref=block, send_sem=zsend.at[h, to], recv_sem=recv.at[h, z, x],
            device_id={"blk": place(to, x, core)}, device_id_type=MESH,
        )

    def x_copy(h, zo, to):
        block = bufs[h].at[zo, x, core]
        return pltpu.make_async_remote_copy(
            src_ref=block, dst_ref=block, send_sem=xsend.at[h, zo, to], recv_sem=recv.at[h, zo, x],
            device_id={"blk": place(z, to, core)}, device_id_type=MESH,
        )

    def c_copy(h, xo, co):
        column = bufs[h].at[:, xo, co]
        return pltpu.make_async_remote_copy(
            src_ref=column, dst_ref=column, send_sem=csend.at[h, xo], recv_sem=crecv.at[h, xo],
            device_id={"blk": sibling}, device_id_type=MESH,
        )

    def arrive(h, zo, xo):
        block = bufs[h].at[zo, xo, core]
        pltpu.make_async_remote_copy(
            src_ref=block, dst_ref=block, send_sem=xsend.at[h, zo, xo], recv_sem=recv.at[h, zo, xo],
            device_id={"blk": sibling}, device_id_type=MESH,
        ).wait_recv()

    def each_x(fn):
        for xo in range(nx):
            @pl.when(xo != x)
            def _(xo=xo):
                fn(xo)

    def each_z(fn):
        for d in range(1, nz):
            for zo in (z - d, z + d):
                @pl.when((zo >= 0) & (zo < nz))
                def _(zo=zo):
                    fn(zo)

    def launch(h):
        each_z(lambda zo: z_copy(h, zo).start())

    def launch_x(h):
        each_x(lambda xo: x_copy(h, z, xo).start())

    launch_x(0)
    launch(0)

    def lagged(t, lag):
        d = t // 2 - lag
        s = 1 - 2 * (t % 2)
        zo = z - s * d
        valid = (d >= 0) & (zo >= 0) & (zo < nz) & ((d > 0) | (s == 1))
        return d, zo, valid

    def forward_z(h, t):
        d, zo, valid = lagged(t, 0)

        @pl.when(valid & (d > 0))
        def _():
            arrive(h, zo, x)
            each_x(lambda xo: x_copy(h, zo, xo).start())

    def receive_x(h, t):
        _, zo, valid = lagged(t, 0)

        @pl.when(valid)
        def _():
            each_x(lambda xo: arrive(h, zo, xo))

    def at(ref, o):
        return ref.at[o // (2 * nx), (o // 2) % nx, o % 2]

    def variance(o):
        tail = at(dbuf, o)[members:].astype(F32)
        return tail[0:1] + tail[1:2] + tail[2:3]

    def absorb_all(places):
        scaled, plain = [], []
        for zo, xo, co in places:
            o = place(zo, xo, co)
            db = dbuf[zo, xo, co, :members]
            tail = dbuf[zo, xo, co, members:].astype(F32)
            sb = (db.astype(F32) * (1.0 / (tail[0:1] + tail[1:2] + tail[2:3]))).astype(BF16)
            sbuf[o] = sb
            scaled.append(sb)
            plain.append(db)
        left, right = jnp.concatenate(scaled, axis=1), jnp.concatenate(plain, axis=1)
        total[...] += lax.dot_general(left, right, NT, preferred_element_type=F32)

    def absorb(zo, xo, co):
        absorb_all([(zo, xo, co)])

    def over_own(t, carry):
        forward_z(0, t)

        @pl.when(t == 2 * nz - 1)
        def _():
            c_copy(0, x, core).start()
            launch(1)
        _, zo, valid = lagged(t, 0)

        @pl.when(valid)
        def _():
            absorb(zo, x, core)
        return carry

    def over_far(t, carry):
        receive_x(0, t)
        return carry

    def send_far(h):
        each_x(lambda xo: c_copy(h, xo, core).start())

    lax.fori_loop(0, 2 * nz, over_own, 0)

    def absorb_column(xo, co):
        for first in range(0, nz, BATCH):
            absorb_all([(zo, xo, co) for zo in range(first, min(first + BATCH, nz))])

    def absorb_sent(xo):
        c_copy(0, xo, 1 - core).wait_recv()
        absorb_column(xo, 1 - core)

    absorb_sent(x)
    lax.fori_loop(0, 2 * nz, over_far, 0)
    send_far(0)
    launch_x(1)
    each_x(lambda xo: absorb_column(xo, core))
    each_x(absorb_sent)

    count = [0]

    def relay(fn, spots):

        def one(t, carry):
            fn(t)
            return carry

        for d in range(nz):
            if spots[d * len(spots) // nz] == count[0]:
                lax.fori_loop(2 * d, 2 * d + 2, one, 0)

    def pause():
        relay(lambda t: forward_z(1, t), Z_SPOTS)
        if count[0] == Z_SPOTS[-1]:
            c_copy(1, x, core).start()
        relay(lambda t: receive_x(1, t), X_SPOTS)
        if count[0] == X_SPOTS[-1]:
            send_far(1)
        count[0] += 1

    row = lax.broadcasted_iota(jnp.int32, total.shape, 0)
    col = lax.broadcasted_iota(jnp.int32, total.shape, 1)
    whole = total[...] + jnp.where(row == col, members - 1.0, 0.0)
    pause()
    inverse = right_of(invert_all(whole, ones[...], pause))

    for xo in range(nx):
        c_copy(1, xo, 1 - core).wait_recv()

    group = min(n, 16)

    def gather_cross(g, carry):
        left = jnp.concatenate([at(rbuf, g * group + i)[...] for i in range(group)], axis=1)
        right = jnp.concatenate([sbuf[g * group + i] for i in range(group)], axis=1)
        product = lax.dot_general(left, right, NT, preferred_element_type=F32)
        total[...] = jnp.where(g == 0, product, total[...] + product)
        return carry

    lax.fori_loop(0, n // group, gather_cross, 0)
    xt = mm(left_of(total[...]), inverse)
    stack = jnp.concatenate(split(xt), axis=0)

    def innovate(g, carry):
        for i in range(0, group, 2):
            o = g * group + i
            d = jnp.concatenate([at(dbuf, o)[:members], at(dbuf, o + 1)[:members]], axis=1)
            r = jnp.concatenate([at(rbuf, o)[...], at(rbuf, o + 1)[...]], axis=1).astype(F32)
            w = jnp.concatenate([variance(o), variance(o + 1)], axis=1)
            w = 1.0 / (w * (members - 1.0))
            parts = mm(stack, d)
            update = parts[:members] + (parts[members : 2 * members] + parts[2 * members :])
            v = ((r - update) * w).astype(BF16)
            sbuf[o] = v[:, :width]
            sbuf[o + 1] = v[:, width:]
        return carry

    def out_copy(o):
        return pltpu.make_async_copy(gbuf.at[o], gains.at[o], out_sem.at[o])

    def gain(g, carry):
        for i in range(group):
            o = g * group + i
            product = lax.dot_general(sbuf[o], at(dbuf, o)[:members], NT, preferred_element_type=F32)
            gbuf[o] = product.astype(BF16)
            out_copy(o).start()
        return carry

    lax.fori_loop(0, n // group, innovate, 0)
    lax.fori_loop(0, n // group, gain, 0)

    def drain(h):
        each_z(lambda zo: z_copy(h, zo).wait_send())

        def over_z(zo, carry):
            each_x(lambda xo: x_copy(h, zo, xo).wait_send())
            return carry
        lax.fori_loop(0, nz, over_z, 0)

        for xo in range(nx):
            c_copy(h, xo, core).wait_send()

    drain(0)
    drain(1)

    def stored(o, carry):
        out_copy(o).wait()
        return carry

    lax.fori_loop(0, n, stored, 0)


def all_gains(n, pred, targ, var):
    nz, nx = chip_grid(n)
    members, width = pred.shape
    hbm = pl.BlockSpec(memory_space=pltpu.HBM)
    sem = pltpu.SemaphoreType.DMA
    return pl.pallas_call(
        functools.partial(gains_kernel, nz, nx),
        out_shape=jax.ShapeDtypeStruct((n + SPARE, members, members), BF16),
        in_specs=[hbm, hbm, hbm],
        out_specs=hbm,
        scratch_shapes=[
            pltpu.VMEM((nz, nx, 2, members + EXTRA, width), BF16),
            pltpu.VMEM((nz, nx, 2, members, width), BF16),
            pltpu.VMEM((n, members, width), BF16),
            pltpu.VMEM((n, members, members), BF16),
            pltpu.VMEM((members, width), BF16),
            pltpu.VMEM((members, width), BF16),
            pltpu.VMEM((1, width), F32),
            pltpu.VMEM((members, members), F32),
            pltpu.VMEM((8, TILE), F32),
            sem((3,)), sem((n,)), sem((2, nz)), sem((2, nz, nx)), sem((2, nx)), sem((2, nz, nx)), sem((2, nx)),
        ],
        compiler_params=pltpu.CompilerParams(
            collective_id=0, has_side_effects=True, vmem_limit_bytes=VMEM
        ),
        name="gather_gains",
    )(pred, targ, var)


def step_kernel(
    ids, far_gains, pair, taper, ens, out,
    gains, mixer, gain_sum, uanom, result, gain_sem, sems,
):
    slots, members, _ = gains.shape
    blocks = pair.shape[0]
    cell = ens.shape[1] // blocks
    piece = members // PIECES
    gain_copies = []
    for k in range(PIECES):
        some = pl.ds(k * piece, piece)
        gain_copies.append(
            pltpu.make_async_copy(far_gains.at[pl.ds(0, slots), some], gains.at[:, some], gain_sem.at[k])
        )
        gain_copies[-1].start()
    pairs = pair[...]
    tapers = taper[...]
    spread = ROWS * slots
    lane = lax.broadcasted_iota(jnp.int32, (blocks, spread), 1)
    weight = jnp.zeros((blocks, spread), F32)
    for s in range(slots):
        hit = jnp.where(pairs == ids[s], tapers, 0.0)
        both = jnp.sum(hit, axis=1, keepdims=True)
        weight = jnp.where(lane // ROWS == s, both, weight)
    sub = lax.broadcasted_iota(jnp.int32, (ROWS, spread), 0)
    spot = lax.broadcasted_iota(jnp.int32, (ROWS, spread), 1) % ROWS == sub
    for c in range(blocks):
        row = jnp.broadcast_to(weight[c : c + 1, :], (ROWS, spread))
        mixer[c * ROWS : (c + 1) * ROWS, :] = jnp.where(spot, row, 0.0).astype(BF16)
    mix = mixer[...]
    strips = members // ROWS
    for c in range(blocks):
        u = ens[:, c * cell : (c + 1) * cell].astype(F32)
        uanom[:, c * cell : (c + 1) * cell] = (u - jnp.mean(u, axis=0, keepdims=True)).astype(BF16)
    for i in range(strips):
        if i * ROWS % piece == 0:
            gain_copies[i * ROWS // piece].wait()
        rows = slice(i * ROWS, (i + 1) * ROWS)
        stack = gains[:, rows, :].reshape(slots * ROWS, members)
        mixed = jnp.dot(mix, stack, preferred_element_type=F32).astype(BF16)
        gain_sum[:, rows, :] = mixed.reshape(blocks, ROWS, members)
    copies = []
    for first in range(0, blocks, TOGETHER):
        for c in range(first, first + TOGETHER):
            cols = slice(c * cell, (c + 1) * cell)
            result[:, cols] = jnp.dot(gain_sum[c], uanom[:, cols], preferred_element_type=F32)
        cols = pl.ds(first * cell, TOGETHER * cell)
        copies.append(pltpu.make_async_copy(result.at[:, cols], out.at[:, cols], sems.at[len(copies)]))
        copies[-1].start()
    for copy in copies:
        copy.wait()


def finish(ensemble, gains, ids, pair, taper):
    members, cells = ensemble.shape
    blocks = pair.shape[0]
    slots = ids.shape[0]
    hbm = pl.BlockSpec(memory_space=pltpu.HBM)
    vmem = pl.BlockSpec(memory_space=pltpu.VMEM)
    return pl.pallas_call(
        step_kernel,
        out_shape=jax.ShapeDtypeStruct((members, cells), F32),
        in_specs=[pl.BlockSpec(memory_space=pltpu.SMEM), hbm, vmem, vmem, vmem],
        out_specs=hbm,
        scratch_shapes=[
            pltpu.VMEM((slots, members, members), BF16),
            pltpu.VMEM((blocks * ROWS, slots * ROWS), BF16),
            pltpu.VMEM((blocks, members, members), BF16),
            pltpu.VMEM((members, cells), BF16),
            pltpu.VMEM((members, cells), F32),
            pltpu.SemaphoreType.DMA((PIECES,)),
            pltpu.SemaphoreType.DMA((blocks // TOGETHER,)),
        ],
        compiler_params=pltpu.CompilerParams(vmem_limit_bytes=48 << 20),
        name="mix_step",
    )(ids, gains, pair, taper, ensemble)


def solution(mesh):
    n = mesh.shape["blk"]

    def per_device(ensemble, predicted, targets, datum_noise_variance, block_ids, pair_blocks, taper):
        gains = all_gains(n, predicted, targets, datum_noise_variance.reshape(1, -1))
        return finish(ensemble, gains, block_ids, pair_blocks, taper)

    in_specs = (
        P(None, ("groups", "blk")),
        P(None, ("groups", "blk")),
        P(None, ("groups", "blk")),
        P(("groups", "blk")),
        P("groups"),
        P(("groups", "blk"), None),
        P(("groups", "blk"), None),
    )
    return jax.shard_map(
        per_device, mesh=mesh, in_specs=in_specs, out_specs=P(None, ("groups", "blk")), check_vma=False
    )
```
